512 devices in a mesh: cls: 32 (over z_hi, y, x), slab: 16 (over z_lo, core).
Axes of the slice: x: 4, y: 4, z: 16 (z_hi: 2, z_lo: 8; z = z_hi * 8 + z_lo), core: 2. Of those that a mesh axis runs over, the one named last changes fastest.
Arguments:
- q_init: bfloat16 [32, 256, 64, 128], P('cls', 'slab'), may hold values from 0.5 to 2
- q_back: bfloat16 [32, 4, 256, 64, 128], P('cls', None, 'slab'), may hold values from 0.5 to 2
- fields: float32 [2, 256, 64, 128], P(None, 'slab'), may hold values from -4 to 4
- lengths: int32 [32], replicated, may hold values from 16 to 63
- steps_count: int32 [32], replicated, may hold values from 64 to 127
- block_types: int32 [32, 4], replicated, may hold values from 0 to 1
Outputs:
- fields_new: float32 [2, 256, 64, 128], P(None, 'slab')
- q_final: bfloat16 [32, 256, 64, 128], P('cls', 'slab')
The draws below stay inside these ranges and needn't reach their ends.
Inputs may be any that keep to these rules, and one draw needn't show every extreme that they name: `steps_count`: steps of each class's whole chain.
All inputs are finite; a program needn't handle non-finite values.
Results may differ from the reference program's by a relative error of at most 0.001.
Values sent between devices are 32-bit elements; how exact they have to be, the bound alone decides.
No kernel may reach another device: no remote copies, remote signals or barrier semaphores. Data moves between devices by JAX's collectives and lax.ppermute only.
A program may use at most 64 MiB of HBM per device.

```python
import math
import jax
import jax.numpy as jnp
from jax import lax

NC = 32
STEPS = 4
NX = 64
NY = 128
NZ = 256


def with_ends(values, key, least, largest):
    place = [jax.random.randint(jax.random.fold_in(key, axis), (), 0, length) for axis, length in enumerate(values.shape)]
    widest = values.shape.index(max(values.shape))
    beside = place[:widest] + [(place[widest] + 1) % values.shape[widest]] + place[widest + 1:]
    return values.at[tuple(place)].set(least).at[tuple(beside)].set(largest)


def block_levels(own_key, dims, split, low, top_value):
    level = 1.0
    for axis_at, parts in split:
        heights = jax.random.uniform(jax.random.fold_in(jax.random.fold_in(own_key, 6), axis_at), (parts,), jnp.float32, low / len(split), top_value / len(split))
        level = level * jnp.repeat(jnp.exp(heights), dims[axis_at] // parts).reshape((-1,) + (1,) * (len(dims) - 1 - axis_at))
    return level


def gaussian(key, shape, scale, reach, shards=(), kind=jnp.bfloat16):
    array = jax.random.normal(key, shape, jnp.float32) * scale
    if len(shards) > 0:
        array = block_levels(key, shape, shards, -0.22, 0.18) * array
    return jnp.clip(array, min=-reach, max=reach).astype(kind)


def setup_inputs(seed: int = 0) -> dict:
    keys = jax.random.split(jax.random.key(seed), 7)
    q_init = jnp.clip(jnp.exp(math.log(2.0) - 1.3862944 * jax.random.uniform(keys[0], (NC, NZ, NX, NY), jnp.float32) ** block_levels(keys[0], (NC, NZ, NX, NY), ((0, 32), (1, 16)), -0.2, 0.2)), 0.5, 2.0).astype(jnp.bfloat16)
    q_back = jnp.clip(jnp.exp(math.log(2.0) - 1.3862944 * jax.random.uniform(keys[1], (NC, STEPS, NZ, NX, NY), jnp.float32) ** block_levels(keys[1], (NC, STEPS, NZ, NX, NY), ((0, 32), (2, 16)), -0.2, 0.2)), 0.5, 2.0).astype(jnp.bfloat16)
    fields = gaussian(keys[2], (2, NZ, NX, NY), 1.0, 4.0, ((1, 16),), jnp.float32)
    lengths = with_ends(jax.random.randint(keys[3], (NC,), 16, 64), jax.random.fold_in(keys[3], 1), 16, 63).astype(jnp.int32)
    steps_count = with_ends(jax.random.randint(keys[4], (NC,), 64, 128), jax.random.fold_in(keys[4], 1), 64, 127).astype(jnp.int32)
    block_types = with_ends(jax.random.randint(keys[5], (NC, STEPS), 0, 2), jax.random.fold_in(keys[5], 1), 0, 1).astype(jnp.int32)
    return dict(q_init=q_init, q_back=q_back, fields=fields, lengths=lengths, steps_count=steps_count, block_types=block_types)


flory_chi = 2.0
stiffness = 1.0
mixing = 0.5
diffusion_scale = 0.125


def beside_sum(weighted):
    padded = jnp.pad(weighted, 1)
    total = padded[2:, 1:-1, 1:-1] + padded[:-2, 1:-1, 1:-1]
    total = total + padded[1:-1, 2:, 1:-1] + padded[1:-1, :-2, 1:-1]
    return total + padded[1:-1, 1:-1, 2:] + padded[1:-1, 1:-1, :-2]


def reference(q_init, q_back, fields, lengths, steps_count, block_types):
    step_size = lengths.astype(jnp.float32) / steps_count.astype(jnp.float32)
    spread = diffusion_scale * step_size
    fraction = lengths.astype(jnp.float32) / jnp.sum(lengths).astype(jnp.float32)
    cells = NZ * NX * NY

    def per_class(density, item):
        start, backward, size_c, spread_c, share_c, types = item
        forward = start.astype(jnp.float32)
        products = []
        for step in range(STEPS):
            chosen = jnp.where(types[step] == 0, fields[0], fields[1])
            half = jnp.exp(-0.5 * size_c * chosen)
            weighted = half * forward
            forward = half * ((1.0 - 6.0 * spread_c) * weighted + spread_c * beside_sum(weighted))
            products.append(forward * backward[step].astype(jnp.float32))
        partition = jnp.sum(products[0]) / cells
        weight = share_c * size_c / partition
        for step in range(STEPS):
            select = (jnp.arange(2, dtype=jnp.int32) == types[step]).astype(jnp.float32)
            density = density + weight * select[:, None, None, None] * products[step][None]
        return density, forward.astype(jnp.bfloat16)

    empty = jnp.zeros((2, NZ, NX, NY), jnp.float32)
    density, q_final = lax.scan(per_class, empty, (q_init, q_back, step_size, spread, fraction, block_types))
    total = density[0] + density[1]
    level = jnp.mean(total)
    pressure = stiffness * (total - level)
    first = fields[0] + mixing * (flory_chi * density[1] + pressure - fields[0])
    second = fields[1] + mixing * (flory_chi * density[0] + pressure - fields[1])
    return jnp.stack([first, second]), q_final
```

```python
import functools

import jax
import jax.numpy as jnp
from jax import lax
from jax.experimental import pallas as pl
from jax.experimental.pallas import tpu as pltpu
from jax.sharding import Mesh
from jax.sharding import PartitionSpec as P

CLS = ("zh", "y", "x")
XY = ("y", "x")
SLAB = "slab"

flory_chi = 2.0
stiffness = 1.0
mixing = 0.5
diffusion_scale = 0.125

VMEM = pl.BlockSpec(memory_space=pltpu.VMEM)
SMEM = pl.BlockSpec(memory_space=pltpu.SMEM)
TOP = 8


def own_class():
    return (lax.axis_index("zh") * 4 + lax.axis_index("y")) * 4 + lax.axis_index("x")


def splat(value, shape=(1, 128)):
    return jnp.full(shape, value, jnp.float32)


def size_of(lengths, counts, cls):
    return splat(lengths[cls].astype(jnp.float32)) / splat(counts[cls].astype(jnp.float32))


def folded(plane):
    return jnp.sum(plane.reshape(-1, 8, plane.shape[-1]), axis=0)


def neighbours(w, slot, p, lane_low, lane_high, nx):
    core = w[slot, p, TOP : TOP + nx, :]
    total = w[slot, p - 1, TOP : TOP + nx, :] + w[slot, p + 1, TOP : TOP + nx, :]
    total = total + w[slot, p, TOP - 1 : TOP + nx - 1, :] + w[slot, p, TOP + 1 : TOP + nx + 1, :]
    ny = core.shape[-1]
    before = jnp.where(lane_low, 0.0, pltpu.roll(core, 1, 1))
    after = jnp.where(lane_high, 0.0, pltpu.roll(core, ny - 1, 1))
    return core, total + before + after


def lane_edges(nx, ny):
    lane = lax.broadcasted_iota(jnp.int32, (nx, ny), 1)
    return lane == 0, lane == ny - 1


def clear_margins(w, nx):
    blank = jnp.zeros(w.shape[:2] + (TOP, w.shape[-1]), jnp.float32)
    w[:, :, 0:TOP, :] = blank
    w[:, :, TOP + nx : TOP + nx + TOP, :] = blank


def partition_kernel(lengths, counts, types, low, high, q, back, fields, out, w, total):
    planes, nx, ny = q.shape
    depth = low.shape[1]
    cls = own_class()
    size = size_of(lengths, counts, cls)
    spread = diffusion_scale * size
    keep = 1.0 - 6.0 * spread
    scale = -0.5 * size
    kind = types[cls, 0]
    edge_low, edge_high = lane_edges(nx, ny)
    clear_margins(w, nx)
    w[0, 0, TOP : TOP + nx, :] = jnp.exp(scale * low[1 + kind, depth - 1]) * low[0, depth - 1]
    w[0, planes + 1, TOP : TOP + nx, :] = jnp.exp(scale * high[1 + kind, 0]) * high[0, 0]

    def weigh(p, carry):
        start = q[p].astype(jnp.float32)
        w[0, p + 1, TOP : TOP + nx, :] = jnp.exp(scale * fields[kind, p]) * start
        return carry

    lax.fori_loop(0, planes, weigh, 0, unroll=2)
    total[...] = jnp.zeros_like(total)

    def step(p, carry):
        core, beside = neighbours(w, 0, p + 1, edge_low, edge_high, nx)
        half = jnp.exp(scale * fields[kind, p])
        fresh = half * (keep * core + spread * beside)
        total[...] += folded(fresh * back[0, p].astype(jnp.float32))
        return carry

    lax.fori_loop(0, planes, step, 0, unroll=2)
    out[...] = jnp.broadcast_to(total[...][None], out.shape)


def main_kernel(
    lengths, counts, types, low, high, q, back, fields, final, dens, sums, half, w, total
):
    planes, nx, ny = q.shape
    depth = low.shape[1]
    wide = planes + 2 * depth
    cls = own_class()
    slab = lax.axis_index(SLAB)
    inner_low = splat(jnp.where(slab > 0, 1.0, 0.0))
    inner_high = splat(jnp.where(slab < lax.axis_size(SLAB) - 1, 1.0, 0.0))
    size = size_of(lengths, counts, cls)
    spread = diffusion_scale * size
    keep = 1.0 - 6.0 * spread
    scale = -0.5 * size
    kinds = [types[cls, s] for s in range(depth)]
    edge_low, edge_high = lane_edges(nx, ny)
    clear_margins(w, nx)
    total[...] = jnp.zeros_like(total)
    rows = slice(TOP, TOP + nx)

    for p in range(depth):
        for t in range(2):
            half[t, p] = jnp.exp(scale * low[1 + t, p])
            half[t, depth + planes + p] = jnp.exp(scale * high[1 + t, p])
        w[0, p, rows, :] = half[kinds[0], p] * low[0, p]
        w[0, depth + planes + p, rows, :] = half[kinds[0], depth + planes + p] * high[0, p]

    def first(p, carry):
        half[0, depth + p] = jnp.exp(scale * fields[0, p])
        half[1, depth + p] = jnp.exp(scale * fields[1, p])
        w[0, depth + p, rows, :] = half[kinds[0], depth + p] * q[p].astype(jnp.float32)
        dens[p, 0] = jnp.zeros((nx, ny), jnp.float32)
        dens[p, 1] = jnp.zeros((nx, ny), jnp.float32)
        return carry

    lax.fori_loop(0, planes, first, 0, unroll=2)

    for s in range(depth):
        now, later = s % 2, (s + 1) % 2
        kind = kinds[s]
        last = s == depth - 1

        def fresh_of(p):
            core, beside = neighbours(w, now, p, edge_low, edge_high, nx)
            return half[kind, p] * (keep * core + spread * beside)

        for p in range(s + 1, depth):
            far = wide - 1 - p
            w[later, p, rows, :] = half[kinds[s + 1], p] * (inner_low * fresh_of(p))
            w[later, far, rows, :] = half[kinds[s + 1], far] * (inner_high * fresh_of(far))

        def middle(p, carry):
            fresh = fresh_of(p + depth)
            product = fresh * back[s, p].astype(jnp.float32)
            dens[p, kind] += product
            total[...] += folded(product)
            if last:
                final[p] = fresh.astype(jnp.bfloat16)
            else:
                w[later, p + depth, rows, :] = half[kinds[s + 1], p + depth] * fresh
            return carry

        lax.fori_loop(0, planes, middle, 0, unroll=2)
    sums[...] = total[...]


def weigh_kernel(cells, lengths, counts, parts, dens, sums, out):
    planes, _, nx, ny = dens.shape
    cls = own_class()
    size = size_of(lengths, counts, cls)
    whole = lengths[0]
    for c in range(1, lengths.shape[0]):
        whole = whole + lengths[c]
    fraction = splat(lengths[cls].astype(jnp.float32)) / splat(whole.astype(jnp.float32))
    partition = jnp.sum(parts[...]) / cells
    weight = fraction * size / splat(partition)
    extra = weight * sums[...]

    def body(p, carry):
        out[p, 0:nx, :] = weight * dens[p, 0]
        out[p, nx : 2 * nx, :] = weight * dens[p, 1]
        out[p, 2 * nx : 2 * nx + 8, :] = extra
        return carry

    lax.fori_loop(0, planes, body, 0, unroll=2)


def reduce_kernel(arrived, out):
    acc = arrived[0]
    for c in range(1, arrived.shape[0]):
        acc = acc + arrived[c]
    out[...] = acc


def spread_kernel(own, other, blocks, levels):
    both = own[...] + other[...]
    n = blocks.shape[1]
    blocks[...] = jnp.broadcast_to(both[None, :n], blocks.shape)
    levels[...] = jnp.broadcast_to(both[None, n:], levels.shape)


def update_kernel(cells, blocks, levels, fields, out):
    _, planes, nx, ny = fields.shape
    level = splat(jnp.sum(levels[...]) / cells)

    def body(p, carry):
        first, second = blocks[p, 0:nx, :], blocks[p, nx : 2 * nx, :]
        pressure = stiffness * (first + second - level)
        old = fields[0, p]
        out[0, p] = old + mixing * (flory_chi * second + pressure - old)
        old = fields[1, p]
        out[1, p] = old + mixing * (flory_chi * first + pressure - old)
        return carry

    lax.fori_loop(0, planes, body, 0, unroll=2)


def call(kernel, outs, scratch, args, smem, flops, name):
    size = sum(a.size * a.dtype.itemsize for a in args) + sum(
        o.size * o.dtype.itemsize for o in outs
    )
    return pl.pallas_call(
        kernel,
        out_shape=outs,
        in_specs=[SMEM] * smem + [VMEM] * (len(args) - smem),
        out_specs=[VMEM] * len(outs),
        scratch_shapes=scratch,
        compiler_params=pltpu.CompilerParams(vmem_limit_bytes=24 * 2**20),
        cost_estimate=pl.CostEstimate(flops=flops, bytes_accessed=size, transcendentals=0),
        name=name,
    )(*args)


def f32(*shape):
    return jax.ShapeDtypeStruct(shape, jnp.float32)


def swapped(x, axis, shift):
    count = lax.axis_size(axis)
    pairs = [(i, i + shift) for i in range(count) if 0 <= i + shift < count]
    return lax.ppermute(x, axis, pairs)


def body(q_init, q_back, fields, lengths, counts, types):
    _, planes, nx, ny = q_init.shape
    depth = q_back.shape[1]
    cells = float(lax.axis_size(SLAB) * planes * nx * ny)
    q, back = q_init[0], q_back[0]
    peers = lax.axis_size(XY)
    slabs = lax.axis_size(SLAB)

    def edge(start):
        own = lax.slice_in_dim(q, start, start + depth, axis=0).astype(jnp.float32)
        return jnp.concatenate(
            [own[None], lax.slice_in_dim(fields, start, start + depth, axis=1)], 0
        )

    low = swapped(edge(planes - depth), SLAB, 1)
    high = swapped(edge(0), SLAB, -1)

    padded = nx + 2 * TOP
    ins = (lengths, counts, types, low, high, q, back, fields)
    (parts,) = call(
        partition_kernel,
        [f32(slabs, 8, ny)],
        [pltpu.VMEM((1, planes + 2, padded, ny), jnp.float32), pltpu.VMEM((8, ny), jnp.float32)],
        ins,
        3,
        10**6,
        "partition",
    )
    parts = lax.all_to_all(parts, SLAB, 0, 0, tiled=True)
    wide = planes + 2 * depth
    final, dens, sums = call(
        main_kernel,
        [
            jax.ShapeDtypeStruct((planes, nx, ny), jnp.bfloat16),
            f32(planes, 2, nx, ny),
            f32(8, ny),
        ],
        [
            pltpu.VMEM((2, wide, nx, ny), jnp.float32),
            pltpu.VMEM((2, wide, padded, ny), jnp.float32),
            pltpu.VMEM((8, ny), jnp.float32),
        ],
        ins,
        3,
        10**8,
        "propagate",
    )
    (sent,) = call(
        functools.partial(weigh_kernel, cells),
        [f32(peers, 2 * nx + 8, ny)],
        [],
        (lengths, counts, parts, dens, sums),
        2,
        10**6,
        "weigh",
    )
    arrived = lax.all_to_all(sent, XY, 0, 0, tiled=True)
    (own,) = call(reduce_kernel, [f32(2 * nx + 8, ny)], [], (arrived,), 0, 10**6, "reduce")
    other = lax.ppermute(own, "zh", [(0, 1), (1, 0)])
    blocks, levels = call(
        spread_kernel,
        [f32(peers, 2 * nx, ny), f32(slabs, 8, ny)],
        [],
        (own, other),
        0,
        10**6,
        "spread",
    )
    levels = lax.all_to_all(levels, SLAB, 0, 0, tiled=True)
    blocks = lax.all_to_all(blocks, XY, 0, 0, tiled=True)
    (fields_new,) = call(
        functools.partial(update_kernel, cells),
        [f32(2, planes, nx, ny)],
        [],
        (blocks, levels, fields),
        0,
        10**6,
        "update",
    )
    return fields_new, final[None]


def solution(mesh):
    finer = Mesh(mesh.devices.reshape(2, 4, 4, mesh.shape["slab"]), ("zh", "y", "x", SLAB))
    in_specs = (
        P(CLS, SLAB, None, None),
        P(CLS, None, SLAB, None, None),
        P(None, SLAB, None, None),
        P(),
        P(),
        P(),
    )
    out_specs = (P(None, SLAB, None, None), P(CLS, SLAB, None, None))
    return jax.shard_map(body, mesh=finer, in_specs=in_specs, out_specs=out_specs, check_vma=False)
```

```python
import functools

import jax
import jax.numpy as jnp
from jax import lax
from jax.experimental import pallas as pl
from jax.experimental.pallas import tpu as pltpu
from jax.sharding import Mesh
from jax.sharding import PartitionSpec as P

CLS = ("zh", "y", "x")
XY = ("y", "x")
SLAB = "slab"

flory_chi = 2.0
stiffness = 1.0
mixing = 0.5
diffusion_scale = 0.125

VMEM = pl.BlockSpec(memory_space=pltpu.VMEM)
SMEM = pl.BlockSpec(memory_space=pltpu.SMEM)
TOP = 8


def own_class():
    return (lax.axis_index("zh") * 4 + lax.axis_index("y")) * 4 + lax.axis_index("x")


def splat(value, shape=(1, 128)):
    return jnp.full(shape, value, jnp.float32)


def size_of(lengths, counts, cls):
    return splat(lengths[cls].astype(jnp.float32)) / splat(counts[cls].astype(jnp.float32))


def folded(plane):
    return jnp.sum(plane.reshape(-1, 8, plane.shape[-1]), axis=0)


def neighbours(w, at, p, lane_low, lane_high, nx):
    core = w[(*at, p, slice(TOP, TOP + nx))]
    total = w[(*at, p - 1, slice(TOP, TOP + nx))] + w[(*at, p + 1, slice(TOP, TOP + nx))]
    total = total + w[(*at, p, slice(TOP - 1, TOP + nx - 1))]
    total = total + w[(*at, p, slice(TOP + 1, TOP + nx + 1))]
    ny = core.shape[-1]
    before = jnp.where(lane_low, 0.0, pltpu.roll(core, 1, 1))
    after = jnp.where(lane_high, 0.0, pltpu.roll(core, ny - 1, 1))
    return core, total + before + after


def lane_edges(nx, ny):
    lane = lax.broadcasted_iota(jnp.int32, (nx, ny), 1)
    return lane == 0, lane == ny - 1


def clear_margins(w, nx):
    blank = jnp.zeros(w.shape[:2] + (TOP, w.shape[-1]), jnp.float32)
    w[:, :, 0:TOP, :] = blank
    w[:, :, TOP + nx : TOP + nx + TOP, :] = blank


def edges_kernel(lengths, counts, types, q, fields, up, down, ends, sems):
    planes = q.shape[0]
    depth = types.shape[0]
    cls = own_class()
    kind = types[0, cls]
    rest = depth - 1
    copies = []
    for side, start in enumerate((planes - depth, 0)):
        copies.append((q.at[pl.ds(start, depth)], ends.at[side]))
    for t in range(2):
        at = pl.ds(depth + t * rest, rest)
        copies.append((fields.at[t, pl.ds(planes - rest, rest)], up.at[at]))
        copies.append((fields.at[t, pl.ds(0, rest)], down.at[at]))
    copies.append((fields.at[kind, pl.ds(planes - depth, 1)], up.at[pl.ds(0, 1)]))
    copies.append((fields.at[kind, pl.ds(rest, 1)], down.at[pl.ds(rest, 1)]))
    copies = [pltpu.make_async_copy(a, b, sems.at[i]) for i, (a, b) in enumerate(copies)]
    for copy in copies:
        copy.start()
    for copy in copies:
        copy.wait()
    scale = -0.5 * size_of(lengths, counts, cls)
    ours = depth + kind * rest
    for p in range(depth):
        chosen = up[0] if p == 0 else up[ours + p - 1]
        up[p] = jnp.exp(scale * chosen) * ends[0, p].astype(jnp.float32)
        chosen = down[rest] if p == rest else down[ours + p]
        down[p] = jnp.exp(scale * chosen) * ends[1, p].astype(jnp.float32)


def inner_kernel(
    lengths, counts, types, q, back, fields, half, state, dens, middle, sums, w, total
):
    planes, nx, ny = q.shape
    depth = back.shape[0]
    cls = own_class()
    size = size_of(lengths, counts, cls)
    spread = diffusion_scale * size
    keep = 1.0 - 6.0 * spread
    scale = -0.5 * size
    kinds = [types[s, cls] for s in range(depth)]
    edge_low, edge_high = lane_edges(nx, ny)
    clear_margins(w, nx)
    total[...] = jnp.zeros_like(total)
    rows = slice(TOP, TOP + nx)

    def first(p, carry):
        half[0, p] = jnp.exp(scale * fields[0, p])
        half[1, p] = jnp.exp(scale * fields[1, p])
        w[0, p, rows, :] = half[kinds[0], p] * q[p].astype(jnp.float32)
        dens[p, 0] = jnp.zeros((nx, ny), jnp.float32)
        dens[p, 1] = jnp.zeros((nx, ny), jnp.float32)
        return carry

    lax.fori_loop(0, planes, first, 0, unroll=2)

    for s in range(depth):
        now, later = s % 2, (s + 1) % 2
        kind = kinds[s]
        last = s == depth - 1
        for i, p in enumerate((s, s + 1, planes - 1 - s, planes - 2 - s)):
            state[s, i] = w[now, p, rows, :]

        def each(p, carry):
            core, beside = neighbours(w, (now,), p, edge_low, edge_high, nx)
            fresh = half[kind, p] * (keep * core + spread * beside)
            product = fresh * back[s, p].astype(jnp.float32)
            dens[p, kind] += product
            total[...] += folded(product)
            if last:
                middle[p - depth] = fresh.astype(jnp.bfloat16)
            else:
                w[later, p, rows, :] = half[kinds[s + 1], p] * fresh
            return carry

        lax.fori_loop(s + 1, planes - 1 - s, each, 0, unroll=2)
        if s == 0:
            sums[0] = total[...]
    sums[1] = total[...]


def outer_kernel(
    lengths,
    counts,
    types,
    low,
    high,
    back,
    half,
    state,
    dens,
    middle,
    inner_sums,
    final,
    edge_dens,
    sums,
    w,
    total,
):
    planes, nx, ny = final.shape
    depth = back.shape[0]
    cls = own_class()
    slab = lax.axis_index(SLAB)
    inside = (
        splat(jnp.where(slab > 0, 1.0, 0.0)),
        splat(jnp.where(slab < lax.axis_size(SLAB) - 1, 1.0, 0.0)),
    )
    size = size_of(lengths, counts, cls)
    spread = diffusion_scale * size
    keep = 1.0 - 6.0 * spread
    scale = -0.5 * size
    kinds = [types[s, cls] for s in range(depth)]
    edge_low, edge_high = lane_edges(nx, ny)
    for side in range(2):
        clear_margins(w.at[side], nx)
    total[...] = jnp.zeros_like(total)
    rows = slice(TOP, TOP + nx)
    came = (low, high)
    rest = depth - 1

    def half_of(side, r, kind):
        if r >= depth:
            return half[kind, r - depth if side == 0 else planes - 1 + depth - r]
        at = r - 1 if side == 0 else rest - r
        return jnp.exp(scale * came[side][depth + kind * rest + at])

    for side in range(2):
        for r in range(depth):
            w[side, 0, r, rows, :] = came[side][r if side == 0 else rest - r]
        for p in range(depth):
            at = p if side == 0 else planes - 1 - p
            for t in range(2):
                edge_dens[side * depth + p, t] = dens[at, t]

    for s in range(depth):
        now, later = s % 2, (s + 1) % 2
        for side in range(2):
            for i in range(2):
                w[side, now, s + depth + i, rows, :] = state[s, 2 * side + i]
        for i in range(depth):
            for side in range(2):
                r = s + 1 + i
                core, beside = neighbours(w, (side, now), r, edge_low, edge_high, nx)
                fresh = half_of(side, r, kinds[s]) * (keep * core + spread * beside)
                if r < depth:
                    fresh = inside[side] * fresh
                else:
                    at = r - depth if side == 0 else planes - 1 + depth - r
                    product = fresh * back[s, at].astype(jnp.float32)
                    edge_dens[side * depth + r - depth, kinds[s]] += product
                    total[...] += folded(product)
                    if s == rest:
                        final[at] = fresh.astype(jnp.bfloat16)
                if s < rest:
                    w[side, later, r, rows, :] = half_of(side, r, kinds[s + 1]) * fresh
        if s == 0:
            part = inner_sums[0] + total[...]
            sums[:, 0:8] = jnp.broadcast_to(part[None], (sums.shape[0], 8, ny))
    whole = inner_sums[1] + total[...]
    sums[:, 8:16] = jnp.broadcast_to(whole[None], (sums.shape[0], 8, ny))
    for p in range(planes - 2 * depth):
        final[depth + p] = middle[p]


def weigh_kernel(cells, lengths, counts, sums, dens, edge_dens, out, extra):
    planes, _, nx, ny = dens.shape
    depth = edge_dens.shape[0] // 2
    cls = own_class()
    size = size_of(lengths, counts, cls)
    whole = lengths[0]
    for c in range(1, lengths.shape[0]):
        whole = whole + lengths[c]
    fraction = splat(lengths[cls].astype(jnp.float32)) / splat(whole.astype(jnp.float32))
    both = jnp.sum(sums[...], axis=0)
    partition = jnp.sum(both[0:8]) / cells
    weight = fraction * size / splat(partition)
    extra[...] = weight * both[8:16]

    def body(p, carry):
        for t in range(2):
            out[p, t * nx : (t + 1) * nx, :] = weight * dens[p, t]
        return carry

    lax.fori_loop(depth, planes - depth, body, 0, unroll=2)

    def ends(p, carry):
        for t in range(2):
            out[p, t * nx : (t + 1) * nx, :] = weight * edge_dens[p, t]
            out[planes - 1 - p, t * nx : (t + 1) * nx, :] = weight * edge_dens[depth + p, t]
        return carry

    lax.fori_loop(0, depth, ends, 0)


def reduce_kernel(arrived, extra, out):
    acc = arrived[0]
    for c in range(1, arrived.shape[0]):
        acc = acc + arrived[c]
    out[0 : acc.shape[0]] = acc
    out[acc.shape[0] :] = extra[...]


def spread_kernel(own, other, blocks):
    both = own[...] + other[...]
    blocks[...] = jnp.broadcast_to(both[None], blocks.shape)


def update_kernel(cells, blocks, fields, out):
    _, planes, nx, ny = fields.shape
    level = splat(jnp.sum(jnp.sum(blocks[:, 2 * nx :], axis=0)) / cells)

    def body(p, carry):
        first, second = blocks[p, 0:nx, :], blocks[p, nx : 2 * nx, :]
        pressure = stiffness * (first + second - level)
        old = fields[0, p]
        out[0, p] = old + mixing * (flory_chi * second + pressure - old)
        old = fields[1, p]
        out[1, p] = old + mixing * (flory_chi * first + pressure - old)
        return carry

    lax.fori_loop(0, planes, body, 0, unroll=2)


def call(kernel, outs, scratch, args, smem, flops, name, vmem=2, hbm=0):
    size = sum(a.size * a.dtype.itemsize for a in args) + sum(
        o.size * o.dtype.itemsize for o in outs
    )
    anywhere = pl.BlockSpec(memory_space=pltpu.HBM)
    return pl.pallas_call(
        kernel,
        out_shape=outs,
        in_specs=[SMEM] * smem + [VMEM] * (len(args) - smem - hbm) + [anywhere] * hbm,
        out_specs=[VMEM] * len(outs),
        scratch_shapes=scratch,
        compiler_params=pltpu.CompilerParams(vmem_limit_bytes=vmem and vmem * 2**20),
        cost_estimate=pl.CostEstimate(flops=flops, bytes_accessed=size, transcendentals=0),
        name=name,
    )(*args)


def f32(*shape):
    return jax.ShapeDtypeStruct(shape, jnp.float32)


def swapped(x, axis, shift):
    count = lax.axis_size(axis)
    pairs = [(i, i + shift) for i in range(count) if 0 <= i + shift < count]
    return lax.ppermute(x, axis, pairs)


def body(q_init, q_back, fields, lengths, counts, types):
    _, planes, nx, ny = q_init.shape
    depth = q_back.shape[1]
    cells = float(lax.axis_size(SLAB) * planes * nx * ny)
    q, back = q_init[0], q_back[0]
    types = types.T
    peers = lax.axis_size(XY)
    slabs = lax.axis_size(SLAB)
    message = f32(3 * depth - 2, nx, ny)

    up, down = call(
        edges_kernel,
        [message, message],
        [pltpu.VMEM((2, depth, nx, ny), jnp.bfloat16), pltpu.SemaphoreType.DMA((8,))],
        (lengths, counts, types, q, fields),
        3,
        10**6,
        "edges",
        vmem=None,
        hbm=2,
    )
    low = swapped(up, SLAB, 1)
    high = swapped(down, SLAB, -1)

    padded = nx + 2 * TOP
    half, state, dens, middle, sums = call(
        inner_kernel,
        [
            f32(2, planes, nx, ny),
            f32(depth, 4, nx, ny),
            f32(planes, 2, nx, ny),
            jax.ShapeDtypeStruct((planes - 2 * depth, nx, ny), jnp.bfloat16),
            f32(2, 8, ny),
        ],
        [
            pltpu.VMEM((2, planes, padded, ny), jnp.float32),
            pltpu.VMEM((8, ny), jnp.float32),
        ],
        (lengths, counts, types, q, back, fields),
        3,
        10**8,
        "inner",
        vmem=8,
    )
    final, edge_dens, sums = call(
        outer_kernel,
        [
            jax.ShapeDtypeStruct((planes, nx, ny), jnp.bfloat16),
            f32(2 * depth, 2, nx, ny),
            f32(slabs, 16, ny),
        ],
        [
            pltpu.VMEM((2, 2, 2 * depth + 2, padded, ny), jnp.float32),
            pltpu.VMEM((8, ny), jnp.float32),
        ],
        (lengths, counts, types, low, high, back, half, state, dens, middle, sums),
        3,
        10**8,
        "outer",
        vmem=8,
    )
    sums = lax.all_to_all(sums, SLAB, 0, 0, tiled=True)
    sent, extra = call(
        functools.partial(weigh_kernel, cells),
        [f32(peers, 2 * nx, ny), f32(8, ny)],
        [],
        (lengths, counts, sums, dens, edge_dens),
        2,
        10**6,
        "weigh",
        vmem=8,
    )
    arrived = lax.all_to_all(sent, XY, 0, 0, tiled=True)
    (own,) = call(
        reduce_kernel, [f32(2 * nx + 8, ny)], [], (arrived, extra), 0, 10**6, "reduce", vmem=8
    )
    other = lax.ppermute(own, "zh", [(0, 1), (1, 0)])
    (blocks,) = call(
        spread_kernel, [f32(peers, 2 * nx + 8, ny)], [], (own, other), 0, 10**6, "spread", vmem=8
    )
    blocks = lax.all_to_all(blocks, XY, 0, 0, tiled=True)
    (fields_new,) = call(
        functools.partial(update_kernel, cells),
        [f32(2, planes, nx, ny)],
        [],
        (blocks, fields),
        0,
        10**6,
        "update",
        vmem=8,
    )
    return fields_new, final[None]


def solution(mesh):
    finer = Mesh(mesh.devices.reshape(2, 4, 4, mesh.shape["slab"]), ("zh", "y", "x", SLAB))
    in_specs = (
        P(CLS, SLAB, None, None),
        P(CLS, None, SLAB, None, None),
        P(None, SLAB, None, None),
        P(),
        P(),
        P(),
    )
    out_specs = (P(None, SLAB, None, None), P(CLS, SLAB, None, None))
    return jax.shard_map(body, mesh=finer, in_specs=in_specs, out_specs=out_specs, check_vma=False)
```

```python
import functools

import jax
import jax.numpy as jnp
from jax import lax
from jax.experimental import pallas as pl
from jax.experimental.pallas import tpu as pltpu
from jax.sharding import Mesh
from jax.sharding import PartitionSpec as P

CLS = ("zh", "y", "x")
XY = ("y", "x")
SLAB = "slab"

flory_chi = 2.0
stiffness = 1.0
mixing = 0.5
diffusion_scale = 0.125

VMEM = pl.BlockSpec(memory_space=pltpu.VMEM)
SMEM = pl.BlockSpec(memory_space=pltpu.SMEM)
UNROLL = True
TOP = 8


def own_class():
    return (lax.axis_index("zh") * 4 + lax.axis_index("y")) * 4 + lax.axis_index("x")


def splat(value, shape=(1, 128)):
    return jnp.full(shape, value, jnp.float32)


def size_of(lengths, counts, cls):
    return splat(lengths[cls].astype(jnp.float32)) / splat(counts[cls].astype(jnp.float32))


def folded(plane):
    return jnp.sum(plane.reshape(-1, 8, plane.shape[-1]), axis=0)


def neighbours(w, at, p, lane_low, lane_high, nx):
    core = w[(*at, p, slice(TOP, TOP + nx))]
    total = w[(*at, p - 1, slice(TOP, TOP + nx))] + w[(*at, p + 1, slice(TOP, TOP + nx))]
    total = total + w[(*at, p, slice(TOP - 1, TOP + nx - 1))]
    total = total + w[(*at, p, slice(TOP + 1, TOP + nx + 1))]
    ny = core.shape[-1]
    before = jnp.where(lane_low, 0.0, pltpu.roll(core, 1, 1))
    after = jnp.where(lane_high, 0.0, pltpu.roll(core, ny - 1, 1))
    return core, total + before + after


def lane_edges(nx, ny):
    lane = lax.broadcasted_iota(jnp.int32, (nx, ny), 1)
    return lane == 0, lane == ny - 1


def clear_margins(w, nx):
    blank = jnp.zeros(w.shape[:2] + (TOP, w.shape[-1]), jnp.float32)
    w[:, :, 0:TOP, :] = blank
    w[:, :, TOP + nx : TOP + nx + TOP, :] = blank


def edges_kernel(lengths, counts, types, q, fields, up, down, ends, sems):
    planes = q.shape[0]
    depth = types.shape[0]
    cls = own_class()
    kind = types[0, cls]
    rest = depth - 1
    copies = []
    for side, start in enumerate((planes - depth, 0)):
        copies.append((q.at[pl.ds(start, depth)], ends.at[side]))
    for t in range(2):
        at = pl.ds(depth + t * rest, rest)
        copies.append((fields.at[t, pl.ds(planes - rest, rest)], up.at[at]))
        copies.append((fields.at[t, pl.ds(0, rest)], down.at[at]))
    copies.append((fields.at[kind, pl.ds(planes - depth, 1)], up.at[pl.ds(0, 1)]))
    copies.append((fields.at[kind, pl.ds(rest, 1)], down.at[pl.ds(rest, 1)]))
    copies = [pltpu.make_async_copy(a, b, sems.at[i]) for i, (a, b) in enumerate(copies)]
    for copy in copies:
        copy.start()
    for copy in copies:
        copy.wait()
    scale = -0.5 * size_of(lengths, counts, cls)
    ours = depth + kind * rest
    for p in range(depth):
        chosen = up[0] if p == 0 else up[ours + p - 1]
        up[p] = jnp.exp(scale * chosen) * ends[0, p].astype(jnp.float32)
        chosen = down[rest] if p == rest else down[ours + p]
        down[p] = jnp.exp(scale * chosen) * ends[1, p].astype(jnp.float32)


def inner_kernel(
    lengths, counts, types, q, back, fields, half, state, dens, middle, sums, w, total
):
    planes, nx, ny = q.shape
    depth = back.shape[0]
    cls = own_class()
    size = size_of(lengths, counts, cls)
    spread = diffusion_scale * size
    keep = 1.0 - 6.0 * spread
    scale = -0.5 * size
    kinds = [types[s, cls] for s in range(depth)]
    edge_low, edge_high = lane_edges(nx, ny)
    clear_margins(w, nx)
    total[...] = jnp.zeros_like(total)
    rows = slice(TOP, TOP + nx)

    def first(p, carry):
        half[0, p] = jnp.exp(scale * fields[0, p])
        half[1, p] = jnp.exp(scale * fields[1, p])
        w[0, p, rows, :] = half[kinds[0], p] * q[p].astype(jnp.float32)
        dens[p, 0] = jnp.zeros((nx, ny), jnp.float32)
        dens[p, 1] = jnp.zeros((nx, ny), jnp.float32)
        return carry

    lax.fori_loop(0, planes, first, 0, unroll=2)

    for s in range(depth):
        now, later = s % 2, (s + 1) % 2
        kind = kinds[s]
        last = s == depth - 1
        for i, p in enumerate((s, s + 1, planes - 1 - s, planes - 2 - s)):
            state[s, i] = w[now, p, rows, :]

        def each(p, carry):
            core, beside = neighbours(w, (now,), p, edge_low, edge_high, nx)
            fresh = half[kind, p] * (keep * core + spread * beside)
            product = fresh * back[s, p].astype(jnp.float32)
            dens[p, kind] += product
            total[...] += folded(product)
            if last:
                middle[p - depth] = fresh.astype(jnp.bfloat16)
            else:
                w[later, p, rows, :] = half[kinds[s + 1], p] * fresh
            return carry

        lax.fori_loop(s + 1, planes - 1 - s, each, 0, unroll=UNROLL)
        if s == 0:
            sums[0] = total[...]
    sums[1] = total[...]


def outer_kernel(
    lengths,
    counts,
    types,
    low,
    high,
    back,
    half,
    state,
    dens,
    middle,
    inner_sums,
    final,
    edge_dens,
    sums,
    w,
    total,
):
    planes, nx, ny = final.shape
    depth = back.shape[0]
    cls = own_class()
    slab = lax.axis_index(SLAB)
    inside = (
        splat(jnp.where(slab > 0, 1.0, 0.0)),
        splat(jnp.where(slab < lax.axis_size(SLAB) - 1, 1.0, 0.0)),
    )
    size = size_of(lengths, counts, cls)
    spread = diffusion_scale * size
    keep = 1.0 - 6.0 * spread
    scale = -0.5 * size
    kinds = [types[s, cls] for s in range(depth)]
    edge_low, edge_high = lane_edges(nx, ny)
    for side in range(2):
        clear_margins(w.at[side], nx)
    total[...] = jnp.zeros_like(total)
    rows = slice(TOP, TOP + nx)
    came = (low, high)
    rest = depth - 1

    def half_of(side, r, kind):
        if r >= depth:
            return half[kind, r - depth if side == 0 else planes - 1 + depth - r]
        at = r - 1 if side == 0 else rest - r
        return jnp.exp(scale * came[side][depth + kind * rest + at])

    for side in range(2):
        for r in range(depth):
            w[side, 0, r, rows, :] = came[side][r if side == 0 else rest - r]
        for p in range(depth):
            at = p if side == 0 else planes - 1 - p
            for t in range(2):
                edge_dens[side * depth + p, t] = dens[at, t]

    for s in range(depth):
        now, later = s % 2, (s + 1) % 2
        for side in range(2):
            for i in range(2):
                w[side, now, s + depth + i, rows, :] = state[s, 2 * side + i]
        for i in range(depth):
            for side in range(2):
                r = s + 1 + i
                core, beside = neighbours(w, (side, now), r, edge_low, edge_high, nx)
                fresh = half_of(side, r, kinds[s]) * (keep * core + spread * beside)
                if r < depth:
                    fresh = inside[side] * fresh
                else:
                    at = r - depth if side == 0 else planes - 1 + depth - r
                    product = fresh * back[s, at].astype(jnp.float32)
                    edge_dens[side * depth + r - depth, kinds[s]] += product
                    total[...] += folded(product)
                    if s == rest:
                        final[at] = fresh.astype(jnp.bfloat16)
                if s < rest:
                    w[side, later, r, rows, :] = half_of(side, r, kinds[s + 1]) * fresh
        if s == 0:
            part = jnp.sum(inner_sums[0] + total[...], axis=0, keepdims=True)
    whole = jnp.sum(inner_sums[1] + total[...], axis=0, keepdims=True)
    both = jnp.concatenate([part, whole], 0)
    sums[...] = jnp.broadcast_to(both[None], sums.shape)
    for p in range(planes - 2 * depth):
        final[depth + p] = middle[p]


def weigh_kernel(cells, lengths, counts, sums, dens, edge_dens, out, extra):
    planes, _, nx, ny = dens.shape
    depth = edge_dens.shape[0] // 2
    cls = own_class()
    size = size_of(lengths, counts, cls)
    whole = lengths[0]
    for c in range(1, lengths.shape[0]):
        whole = whole + lengths[c]
    fraction = splat(lengths[cls].astype(jnp.float32)) / splat(whole.astype(jnp.float32))
    both = jnp.sum(sums[...], axis=0)
    partition = jnp.sum(both[0:1]) / cells
    weight = fraction * size / splat(partition)
    first_row = lax.broadcasted_iota(jnp.int32, extra.shape, 0) == 0
    extra[...] = jnp.where(first_row, weight * both[1:2], 0.0)

    def body(p, carry):
        for t in range(2):
            out[p, t * nx : (t + 1) * nx, :] = weight * dens[p, t]
        return carry

    lax.fori_loop(depth, planes - depth, body, 0, unroll=2)

    def ends(p, carry):
        for t in range(2):
            out[p, t * nx : (t + 1) * nx, :] = weight * edge_dens[p, t]
            out[planes - 1 - p, t * nx : (t + 1) * nx, :] = weight * edge_dens[depth + p, t]
        return carry

    lax.fori_loop(0, depth, ends, 0)


def reduce_kernel(arrived, extra, out):
    acc = arrived[0]
    for c in range(1, arrived.shape[0]):
        acc = acc + arrived[c]
    out[0 : acc.shape[0]] = acc
    out[acc.shape[0] :] = extra[...]


def spread_kernel(own, other, blocks):
    both = own[...] + other[...]
    blocks[...] = jnp.broadcast_to(both[None], blocks.shape)


def update_kernel(cells, blocks, fields, out):
    _, planes, nx, ny = fields.shape
    level = splat(jnp.sum(jnp.sum(blocks[:, 2 * nx :], axis=0)) / cells)

    def body(p, carry):
        first, second = blocks[p, 0:nx, :], blocks[p, nx : 2 * nx, :]
        pressure = stiffness * (first + second - level)
        old = fields[0, p]
        out[0, p] = old + mixing * (flory_chi * second + pressure - old)
        old = fields[1, p]
        out[1, p] = old + mixing * (flory_chi * first + pressure - old)
        return carry

    lax.fori_loop(0, planes, body, 0, unroll=2)


def call(kernel, outs, scratch, args, smem, flops, name, vmem=2, hbm=0):
    size = sum(a.size * a.dtype.itemsize for a in args) + sum(
        o.size * o.dtype.itemsize for o in outs
    )
    anywhere = pl.BlockSpec(memory_space=pltpu.HBM)
    return pl.pallas_call(
        kernel,
        out_shape=outs,
        in_specs=[SMEM] * smem + [VMEM] * (len(args) - smem - hbm) + [anywhere] * hbm,
        out_specs=[VMEM] * len(outs),
        scratch_shapes=scratch,
        compiler_params=pltpu.CompilerParams(vmem_limit_bytes=vmem and vmem * 2**20),
        cost_estimate=pl.CostEstimate(flops=flops, bytes_accessed=size, transcendentals=0),
        name=name,
    )(*args)


def f32(*shape):
    return jax.ShapeDtypeStruct(shape, jnp.float32)


def swapped(x, axis, shift):
    count = lax.axis_size(axis)
    pairs = [(i, i + shift) for i in range(count) if 0 <= i + shift < count]
    return lax.ppermute(x, axis, pairs)


def body(q_init, q_back, fields, lengths, counts, types):
    _, planes, nx, ny = q_init.shape
    depth = q_back.shape[1]
    cells = float(lax.axis_size(SLAB) * planes * nx * ny)
    q, back = q_init[0], q_back[0]
    types = types.T
    peers = lax.axis_size(XY)
    slabs = lax.axis_size(SLAB)
    message = f32(3 * depth - 2, nx, ny)

    up, down = call(
        edges_kernel,
        [message, message],
        [pltpu.VMEM((2, depth, nx, ny), jnp.bfloat16), pltpu.SemaphoreType.DMA((8,))],
        (lengths, counts, types, q, fields),
        3,
        10**6,
        "edges",
        vmem=None,
        hbm=2,
    )
    low = swapped(up, SLAB, 1)
    high = swapped(down, SLAB, -1)

    padded = nx + 2 * TOP
    half, state, dens, middle, sums = call(
        inner_kernel,
        [
            f32(2, planes, nx, ny),
            f32(depth, 4, nx, ny),
            f32(planes, 2, nx, ny),
            jax.ShapeDtypeStruct((planes - 2 * depth, nx, ny), jnp.bfloat16),
            f32(2, 8, ny),
        ],
        [
            pltpu.VMEM((2, planes, padded, ny), jnp.float32),
            pltpu.VMEM((8, ny), jnp.float32),
        ],
        (lengths, counts, types, q, back, fields),
        3,
        10**8,
        "inner",
        vmem=8,
    )
    final, edge_dens, sums = call(
        outer_kernel,
        [
            jax.ShapeDtypeStruct((planes, nx, ny), jnp.bfloat16),
            f32(2 * depth, 2, nx, ny),
            f32(slabs, 2, ny),
        ],
        [
            pltpu.VMEM((2, 2, 2 * depth + 2, padded, ny), jnp.float32),
            pltpu.VMEM((8, ny), jnp.float32),
        ],
        (lengths, counts, types, low, high, back, half, state, dens, middle, sums),
        3,
        10**8,
        "outer",
        vmem=8,
    )
    sums = lax.all_to_all(sums, SLAB, 0, 0, tiled=True)
    sent, extra = call(
        functools.partial(weigh_kernel, cells),
        [f32(peers, 2 * nx, ny), f32(8, ny)],
        [],
        (lengths, counts, sums, dens, edge_dens),
        2,
        10**6,
        "weigh",
        vmem=8,
    )
    arrived = lax.all_to_all(sent, XY, 0, 0, tiled=True)
    (own,) = call(
        reduce_kernel, [f32(2 * nx + 8, ny)], [], (arrived, extra), 0, 10**6, "reduce", vmem=8
    )
    other = lax.ppermute(own, "zh", [(0, 1), (1, 0)])
    (blocks,) = call(
        spread_kernel, [f32(peers, 2 * nx + 8, ny)], [], (own, other), 0, 10**6, "spread", vmem=8
    )
    blocks = lax.all_to_all(blocks, XY, 0, 0, tiled=True)
    (fields_new,) = call(
        functools.partial(update_kernel, cells),
        [f32(2, planes, nx, ny)],
        [],
        (blocks, fields),
        0,
        10**6,
        "update",
        vmem=8,
    )
    return fields_new, final[None]


def solution(mesh):
    finer = Mesh(mesh.devices.reshape(2, 4, 4, mesh.shape["slab"]), ("zh", "y", "x", SLAB))
    in_specs = (
        P(CLS, SLAB, None, None),
        P(CLS, None, SLAB, None, None),
        P(None, SLAB, None, None),
        P(),
        P(),
        P(),
    )
    out_specs = (P(None, SLAB, None, None), P(CLS, SLAB, None, None))
    return jax.shard_map(body, mesh=finer, in_specs=in_specs, out_specs=out_specs, check_vma=False)
```

```python
import functools

import jax
import jax.numpy as jnp
from jax import lax
from jax.experimental import pallas as pl
from jax.experimental.pallas import tpu as pltpu
from jax.sharding import Mesh
from jax.sharding import PartitionSpec as P

CLS = ("zh", "y", "x")
XY = ("y", "x")
SLAB = "slab"

flory_chi = 2.0
stiffness = 1.0
mixing = 0.5
diffusion_scale = 0.125

VMEM = pl.BlockSpec(memory_space=pltpu.VMEM)
SMEM = pl.BlockSpec(memory_space=pltpu.SMEM)
UNROLL = True
TOP = 8


def own_class():
    return (lax.axis_index("zh") * 4 + lax.axis_index("y")) * 4 + lax.axis_index("x")


def splat(value, shape=(1, 128)):
    return jnp.full(shape, value, jnp.float32)


def size_of(lengths, counts, cls):
    return splat(lengths[cls].astype(jnp.float32)) / splat(counts[cls].astype(jnp.float32))


def folded(plane):
    return jnp.sum(plane.reshape(-1, 8, plane.shape[-1]), axis=0)


def neighbours(w, at, p, lane_low, lane_high, nx):
    core = w[(*at, p, slice(TOP, TOP + nx))]
    total = w[(*at, p - 1, slice(TOP, TOP + nx))] + w[(*at, p + 1, slice(TOP, TOP + nx))]
    total = total + w[(*at, p, slice(TOP - 1, TOP + nx - 1))]
    total = total + w[(*at, p, slice(TOP + 1, TOP + nx + 1))]
    ny = core.shape[-1]
    before = jnp.where(lane_low, 0.0, pltpu.roll(core, 1, 1))
    after = jnp.where(lane_high, 0.0, pltpu.roll(core, ny - 1, 1))
    return core, total + before + after


def lane_edges(nx, ny):
    lane = lax.broadcasted_iota(jnp.int32, (nx, ny), 1)
    return lane == 0, lane == ny - 1


def clear_margins(w, nx):
    blank = jnp.zeros(w.shape[:2] + (TOP, w.shape[-1]), jnp.float32)
    w[:, :, 0:TOP, :] = blank
    w[:, :, TOP + nx : TOP + nx + TOP, :] = blank


def sides():
    core = lax.rem(lax.axis_index(SLAB), 2)
    return core, 1 - core


def edges_kernel(lengths, counts, types, q, fields, outward, inward, ends, sems):
    planes = q.shape[0]
    depth = types.shape[0]
    cls = own_class()
    kind = types[0, cls]
    rest = depth - 1
    messages = (outward, inward)
    copies = []
    for m, upper in enumerate(sides()):
        start, turn = upper * (planes - depth) + (1 - upper) * rest, 2 * upper - 1
        for r in range(depth):
            at = start + turn * r
            copies.append((q.at[at], ends.at[m, r]))
            if r == 0:
                copies.append((fields.at[kind, at], messages[m].at[0]))
            else:
                for t in range(2):
                    copies.append((fields.at[t, at], messages[m].at[depth + t * rest + r - 1]))
    copies = [pltpu.make_async_copy(a, b, sems.at[i]) for i, (a, b) in enumerate(copies)]
    for copy in copies:
        copy.start()
    scale = -0.5 * size_of(lengths, counts, cls)
    for copy in copies:
        copy.wait()
    ours = depth + kind * rest
    for m, message in enumerate(messages):
        for r in range(depth):
            chosen = message[0] if r == 0 else message[ours + r - 1]
            message[r] = jnp.exp(scale * chosen) * ends[m, r].astype(jnp.float32)


def inner_kernel(
    lengths, counts, types, q, back, fields, half, state, dens, middle, sums, w, total
):
    planes, nx, ny = q.shape
    depth = back.shape[0]
    cls = own_class()
    size = size_of(lengths, counts, cls)
    spread = diffusion_scale * size
    keep = 1.0 - 6.0 * spread
    scale = -0.5 * size
    kinds = [types[s, cls] for s in range(depth)]
    edge_low, edge_high = lane_edges(nx, ny)
    clear_margins(w, nx)
    total[...] = jnp.zeros_like(total)
    rows = slice(TOP, TOP + nx)

    def first(p, carry):
        half[0, p] = jnp.exp(scale * fields[0, p])
        half[1, p] = jnp.exp(scale * fields[1, p])
        w[0, p, rows, :] = half[kinds[0], p] * q[p].astype(jnp.float32)
        dens[p, 0] = jnp.zeros((nx, ny), jnp.float32)
        dens[p, 1] = jnp.zeros((nx, ny), jnp.float32)
        return carry

    lax.fori_loop(0, planes, first, 0, unroll=2)

    for s in range(depth):
        now, later = s % 2, (s + 1) % 2
        kind = kinds[s]
        last = s == depth - 1
        for i, p in enumerate((s, s + 1, planes - 1 - s, planes - 2 - s)):
            state[s, i] = w[now, p, rows, :]

        def each(p, carry):
            core, beside = neighbours(w, (now,), p, edge_low, edge_high, nx)
            fresh = half[kind, p] * (keep * core + spread * beside)
            product = fresh * back[s, p].astype(jnp.float32)
            dens[p, kind] += product
            total[...] += folded(product)
            if last:
                middle[p - depth] = fresh.astype(jnp.bfloat16)
            else:
                w[later, p, rows, :] = half[kinds[s + 1], p] * fresh
            return carry

        lax.fori_loop(s + 1, planes - 1 - s, each, 0, unroll=UNROLL)
        if s == 0:
            sums[0] = total[...]
    sums[1] = total[...]


def outer_kernel(
    lengths,
    counts,
    types,
    outer,
    near,
    back,
    half,
    state,
    dens,
    middle,
    inner_sums,
    final,
    edge_dens,
    sums,
    w,
    total,
):
    planes, nx, ny = final.shape
    depth = back.shape[0]
    cls = own_class()
    slab = lax.axis_index(SLAB)
    inside = jnp.logical_and(slab > 0, slab < lax.axis_size(SLAB) - 1)
    inside = splat(jnp.where(inside, 1.0, 0.0))
    size = size_of(lengths, counts, cls)
    spread = diffusion_scale * size
    keep = 1.0 - 6.0 * spread
    scale = -0.5 * size
    kinds = [types[s, cls] for s in range(depth)]
    edge_low, edge_high = lane_edges(nx, ny)
    for side in range(2):
        clear_margins(w.at[side], nx)
    total[...] = jnp.zeros_like(total)
    rows = slice(TOP, TOP + nx)
    came = (outer, near)
    rest = depth - 1
    upper = sides()

    def place(m, r):
        return upper[m] * (planes - 1) + (1 - 2 * upper[m]) * (r - depth)

    def half_of(m, r, kind):
        if r >= depth:
            return half[kind, place(m, r)]
        return jnp.exp(scale * came[m][depth + kind * rest + r - 1])

    for m in range(2):
        for r in range(depth):
            w[m, 0, r, rows, :] = came[m][r]
        for p in range(depth):
            for t in range(2):
                edge_dens[upper[m] * depth + p, t] = dens[place(m, depth + p), t]

    for s in range(depth):
        now, later = s % 2, (s + 1) % 2
        for m in range(2):
            for i in range(2):
                w[m, now, s + depth + i, rows, :] = state[s, 2 * upper[m] + i]
        for i in range(depth):
            for m in range(2):
                r = s + 1 + i
                core, beside = neighbours(w, (m, now), r, edge_low, edge_high, nx)
                fresh = half_of(m, r, kinds[s]) * (keep * core + spread * beside)
                if r >= depth:
                    at = place(m, r)
                    product = fresh * back[s, at].astype(jnp.float32)
                    edge_dens[upper[m] * depth + r - depth, kinds[s]] += product
                    total[...] += folded(product)
                    if s == rest:
                        final[at] = fresh.astype(jnp.bfloat16)
                elif m == 0:
                    fresh = inside * fresh
                if s < rest:
                    w[m, later, r, rows, :] = half_of(m, r, kinds[s + 1]) * fresh
        if s == 0:
            part = jnp.sum(inner_sums[0] + total[...], axis=0, keepdims=True)
    whole = jnp.sum(inner_sums[1] + total[...], axis=0, keepdims=True)
    both = jnp.concatenate([part, whole], 0)
    sums[...] = jnp.broadcast_to(both[None], sums.shape)
    for p in range(planes - 2 * depth):
        final[depth + p] = middle[p]


def weigh_kernel(cells, lengths, counts, sums, dens, edge_dens, out, extra):
    planes, _, nx, ny = dens.shape
    depth = edge_dens.shape[0] // 2
    cls = own_class()
    size = size_of(lengths, counts, cls)
    whole = lengths[0]
    for c in range(1, lengths.shape[0]):
        whole = whole + lengths[c]
    fraction = splat(lengths[cls].astype(jnp.float32)) / splat(whole.astype(jnp.float32))
    both = jnp.sum(sums[...], axis=0)
    partition = jnp.sum(both[0:1]) / cells
    weight = fraction * size / splat(partition)
    first_row = lax.broadcasted_iota(jnp.int32, extra.shape, 0) == 0
    extra[...] = jnp.where(first_row, weight * both[1:2], 0.0)

    def body(p, carry):
        for t in range(2):
            out[p, t * nx : (t + 1) * nx, :] = weight * dens[p, t]
        return carry

    lax.fori_loop(depth, planes - depth, body, 0, unroll=2)

    def ends(p, carry):
        for t in range(2):
            out[p, t * nx : (t + 1) * nx, :] = weight * edge_dens[p, t]
            out[planes - 1 - p, t * nx : (t + 1) * nx, :] = weight * edge_dens[depth + p, t]
        return carry

    lax.fori_loop(0, depth, ends, 0)


def reduce_kernel(arrived, extra, out):
    acc = arrived[0]
    for c in range(1, arrived.shape[0]):
        acc = acc + arrived[c]
    out[0 : acc.shape[0]] = acc
    out[acc.shape[0] :] = extra[...]


def spread_kernel(pair, blocks):
    both = pair[0] + pair[1]
    blocks[...] = jnp.broadcast_to(both[None], blocks.shape)


def update_kernel(cells, blocks, fields, out):
    _, planes, nx, ny = fields.shape
    level = splat(jnp.sum(jnp.sum(blocks[:, 2 * nx :], axis=0)) / cells)

    def body(p, carry):
        first, second = blocks[p, 0:nx, :], blocks[p, nx : 2 * nx, :]
        pressure = stiffness * (first + second - level)
        old = fields[0, p]
        out[0, p] = old + mixing * (flory_chi * second + pressure - old)
        old = fields[1, p]
        out[1, p] = old + mixing * (flory_chi * first + pressure - old)
        return carry

    lax.fori_loop(0, planes, body, 0, unroll=2)


def call(kernel, outs, scratch, args, smem, flops, name, vmem=2, hbm=0):
    size = sum(a.size * a.dtype.itemsize for a in args) + sum(
        o.size * o.dtype.itemsize for o in outs
    )
    anywhere = pl.BlockSpec(memory_space=pltpu.HBM)
    return pl.pallas_call(
        kernel,
        out_shape=outs,
        in_specs=[SMEM] * smem + [VMEM] * (len(args) - smem - hbm) + [anywhere] * hbm,
        out_specs=[VMEM] * len(outs),
        scratch_shapes=scratch,
        compiler_params=pltpu.CompilerParams(vmem_limit_bytes=vmem and vmem * 2**20),
        cost_estimate=pl.CostEstimate(flops=flops, bytes_accessed=size, transcendentals=0),
        name=name,
    )(*args)


def f32(*shape):
    return jax.ShapeDtypeStruct(shape, jnp.float32)


def body(q_init, q_back, fields, lengths, counts, types):
    _, planes, nx, ny = q_init.shape
    depth = q_back.shape[1]
    cells = float(lax.axis_size(SLAB) * planes * nx * ny)
    q, back = q_init[0], q_back[0]
    types = types.T
    peers = lax.axis_size(XY)
    slabs = lax.axis_size(SLAB)
    message = f32(3 * depth - 2, nx, ny)

    outward, inward = call(
        edges_kernel,
        [message, message],
        [pltpu.VMEM((2, depth, nx, ny), jnp.bfloat16), pltpu.SemaphoreType.DMA((2 * (3 * depth - 1),))],
        (lengths, counts, types, q, fields),
        3,
        10**6,
        "edges",
        vmem=None,
        hbm=2,
    )
    across = [(i, i + 1) for i in range(1, slabs - 1, 2)]
    within = [(i, i + 1) for i in range(0, slabs, 2)]
    outer = lax.ppermute(outward, SLAB, across + [(b, a) for a, b in across])
    near = lax.ppermute(inward, SLAB, within + [(b, a) for a, b in within])

    padded = nx + 2 * TOP
    half, state, dens, middle, sums = call(
        inner_kernel,
        [
            f32(2, planes, nx, ny),
            f32(depth, 4, nx, ny),
            f32(planes, 2, nx, ny),
            jax.ShapeDtypeStruct((planes - 2 * depth, nx, ny), jnp.bfloat16),
            f32(2, 8, ny),
        ],
        [
            pltpu.VMEM((2, planes, padded, ny), jnp.float32),
            pltpu.VMEM((8, ny), jnp.float32),
        ],
        (lengths, counts, types, q, back, fields),
        3,
        10**8,
        "inner",
        vmem=8,
    )
    final, edge_dens, sums = call(
        outer_kernel,
        [
            jax.ShapeDtypeStruct((planes, nx, ny), jnp.bfloat16),
            f32(2 * depth, 2, nx, ny),
            f32(slabs, 2, ny),
        ],
        [
            pltpu.VMEM((2, 2, 2 * depth + 2, padded, ny), jnp.float32),
            pltpu.VMEM((8, ny), jnp.float32),
        ],
        (lengths, counts, types, outer, near, back, half, state, dens, middle, sums),
        3,
        10**8,
        "outer",
        vmem=8,
    )
    sums = lax.all_to_all(sums, SLAB, 0, 0, tiled=True)
    sent, extra = call(
        functools.partial(weigh_kernel, cells),
        [f32(peers, 2 * nx, ny), f32(8, ny)],
        [],
        (lengths, counts, sums, dens, edge_dens),
        2,
        10**6,
        "weigh",
        vmem=8,
    )
    arrived = lax.all_to_all(sent, XY, 0, 0, tiled=True)
    (own,) = call(
        reduce_kernel, [f32(2 * nx + 8, ny)], [], (arrived, extra), 0, 10**6, "reduce", vmem=8
    )
    pair = lax.all_gather(own, "zh", axis=0, tiled=False)
    (blocks,) = call(
        spread_kernel, [f32(peers, 2 * nx + 8, ny)], [], (pair,), 0, 10**6, "spread", vmem=8
    )
    blocks = lax.all_to_all(blocks, XY, 0, 0, tiled=True)
    (fields_new,) = call(
        functools.partial(update_kernel, cells),
        [f32(2, planes, nx, ny)],
        [],
        (blocks, fields),
        0,
        10**6,
        "update",
        vmem=8,
    )
    return fields_new, final[None]


def solution(mesh):
    finer = Mesh(mesh.devices.reshape(2, 4, 4, mesh.shape["slab"]), ("zh", "y", "x", SLAB))
    in_specs = (
        P(CLS, SLAB, None, None),
        P(CLS, None, SLAB, None, None),
        P(None, SLAB, None, None),
        P(),
        P(),
        P(),
    )
    out_specs = (P(None, SLAB, None, None), P(CLS, SLAB, None, None))
    return jax.shard_map(body, mesh=finer, in_specs=in_specs, out_specs=out_specs, check_vma=False)
```

```python
import functools

import jax
import jax.numpy as jnp
from jax import lax
from jax.experimental import pallas as pl
from jax.experimental.pallas import tpu as pltpu
from jax.sharding import Mesh
from jax.sharding import PartitionSpec as P

CLS = ("zh", "y", "x")
XY = ("y", "x")
SLAB = "slab"

flory_chi = 2.0
stiffness = 1.0
mixing = 0.5
diffusion_scale = 0.125

VMEM = pl.BlockSpec(memory_space=pltpu.VMEM)
SMEM = pl.BlockSpec(memory_space=pltpu.SMEM)
UNROLL = True
TOP = 8


def own_class():
    return (lax.axis_index("zh") * 4 + lax.axis_index("y")) * 4 + lax.axis_index("x")


def splat(value, shape=(1, 128)):
    return jnp.full(shape, value, jnp.float32)


def folded(plane):
    return jnp.sum(plane.reshape(-1, 8, plane.shape[-1]), axis=0)


def neighbours(w, at, p, lane_low, lane_high, nx):
    core = w[(*at, p, slice(TOP, TOP + nx))]
    total = w[(*at, p - 1, slice(TOP, TOP + nx))] + w[(*at, p + 1, slice(TOP, TOP + nx))]
    total = total + w[(*at, p, slice(TOP - 1, TOP + nx - 1))]
    total = total + w[(*at, p, slice(TOP + 1, TOP + nx + 1))]
    ny = core.shape[-1]
    before = jnp.where(lane_low, 0.0, pltpu.roll(core, 1, 1))
    after = jnp.where(lane_high, 0.0, pltpu.roll(core, ny - 1, 1))
    return core, total + before + after


def lane_edges(nx, ny):
    lane = lax.broadcasted_iota(jnp.int32, (nx, ny), 1)
    return lane == 0, lane == ny - 1


def clear_margins(w, nx):
    blank = jnp.zeros(w.shape[:2] + (TOP, w.shape[-1]), jnp.float32)
    w[:, :, 0:TOP, :] = blank
    w[:, :, TOP + nx : TOP + nx + TOP, :] = blank


def sides():
    core = lax.rem(lax.axis_index(SLAB), 2)
    return core, 1 - core


def edges_kernel(
    lengths,
    counts,
    types,
    q,
    fields,
    outward,
    inward,
    params,
    kinds,
    ends,
    raw,
    own_lengths,
    own_counts,
    own_types,
    sems,
):
    planes = q.shape[0]
    depth = types.shape[0]
    cls = own_class()
    messages = (outward, inward)
    copies = [(lengths, own_lengths), (counts, own_counts), (types, own_types)]
    for m, upper in enumerate(sides()):
        start, turn = upper * (planes - depth) + (1 - upper) * (depth - 1), 2 * upper - 1
        for r in range(depth):
            at = start + turn * r
            copies.append((q.at[at], ends.at[m, r]))
            for t in range(2):
                to = raw.at[m, 2 * r + t] if r < 2 else messages[m].at[depth + 1 + 2 * (r - 2) + t]
                copies.append((fields.at[t, at], to))
    copies = [pltpu.make_async_copy(a, b, sems.at[i]) for i, (a, b) in enumerate(copies)]
    for copy in copies:
        copy.start()
    for copy in copies[:3]:
        copy.wait()
    whole = own_lengths[0]
    for c in range(1, own_lengths.shape[0]):
        whole = whole + own_lengths[c]
    length = splat(own_lengths[cls].astype(jnp.float32))
    size = length / splat(own_counts[cls].astype(jnp.float32))
    fraction = length / splat(whole.astype(jnp.float32))
    params[0:1] = size
    params[1:2] = fraction * size
    for s in range(depth):
        kinds[s] = own_types[s, cls]
    first, second = own_types[0, cls], own_types[1, cls]
    scale = -0.5 * size
    for copy in copies[3:]:
        copy.wait()
    for m, message in enumerate(messages):
        for r in range(depth):
            chosen = raw[m, 2 * r + first] if r < 2 else message[depth + 1 + 2 * (r - 2) + first]
            message[r] = jnp.exp(scale * chosen) * ends[m, r].astype(jnp.float32)
        message[depth] = jnp.exp(scale * (raw[m, 2 + first] + raw[m, 2 + second]))


def inner_kernel(
    kinds, params, q, fields, source, half, state, dens, middle, sums, margin, w, total, back, sems
):
    planes, nx, ny = q.shape
    depth = back.shape[0]
    copies = [pltpu.make_async_copy(source.at[s], back.at[s], sems.at[s]) for s in range(depth)]
    for copy in copies:
        copy.start()
    size = params[0:1]
    spread = diffusion_scale * size
    keep = 1.0 - 6.0 * spread
    scale = -0.5 * size
    kinds = [kinds[s] for s in range(depth)]
    edge_low, edge_high = lane_edges(nx, ny)
    clear_margins(w, nx)
    total[...] = jnp.zeros_like(total)
    rows = slice(TOP, TOP + nx)

    def first(p, carry):
        half[0, p] = jnp.exp(scale * fields[0, p])
        half[1, p] = jnp.exp(scale * fields[1, p])
        w[0, p, rows, :] = half[kinds[0], p] * q[p].astype(jnp.float32)
        dens[p, 0] = jnp.zeros((nx, ny), jnp.float32)
        dens[p, 1] = jnp.zeros((nx, ny), jnp.float32)
        return carry

    lax.fori_loop(0, planes, first, 0, unroll=2)

    for s in range(depth):
        now, later = s % 2, (s + 1) % 2
        kind = kinds[s]
        last = s == depth - 1
        copies[s].wait()
        for i, p in enumerate((s, s + 1, planes - 1 - s, planes - 2 - s)):
            state[s, i] = w[now, p, rows, :]

        def each(p, carry):
            core, beside = neighbours(w, (now,), p, edge_low, edge_high, nx)
            fresh = half[kind, p] * (keep * core + spread * beside)
            product = fresh * back[s, p].astype(jnp.float32)
            dens[p, kind] += product
            total[...] += folded(product)
            if last:
                middle[p - depth] = fresh.astype(jnp.bfloat16)
            else:
                w[later, p, rows, :] = half[kinds[s + 1], p] * fresh
            return carry

        lax.fori_loop(s + 1, planes - 1 - s, each, 0, unroll=UNROLL)
        if s == 0:
            sums[0] = total[...]
        for p in range(depth):
            margin[s, p] = back[s, p]
            margin[s, depth + p] = back[s, planes - 1 - p]
    sums[1] = total[...]


def outer_kernel(
    kinds,
    params,
    outer,
    near,
    half,
    state,
    dens,
    middle,
    inner_sums,
    margin,
    final,
    edge_dens,
    sums,
    w,
    total,
):
    planes, nx, ny = final.shape
    depth = margin.shape[0]
    slab = lax.axis_index(SLAB)
    inside = jnp.logical_and(slab > 0, slab < lax.axis_size(SLAB) - 1)
    inside = splat(jnp.where(inside, 1.0, 0.0))
    size = params[0:1]
    spread = diffusion_scale * size
    keep = 1.0 - 6.0 * spread
    scale = -0.5 * size
    kinds = [kinds[s] for s in range(depth)]
    edge_low, edge_high = lane_edges(nx, ny)
    for side in range(2):
        clear_margins(w.at[side], nx)
    total[...] = jnp.zeros_like(total)
    rows = slice(TOP, TOP + nx)
    came = (outer, near)
    rest = depth - 1
    upper = sides()

    def place(m, r):
        return upper[m] * (planes - 1) + (1 - 2 * upper[m]) * (r - depth)

    def half_of(m, r, kind):
        if r >= depth:
            return half[kind, place(m, r)]
        return jnp.exp(scale * came[m][depth + 1 + 2 * (r - 2) + kind])

    for m in range(2):
        for r in range(depth):
            w[m, 0, r, rows, :] = came[m][r]
        for p in range(depth):
            for t in range(2):
                edge_dens[upper[m] * depth + p, t] = dens[place(m, depth + p), t]

    for s in range(depth):
        now, later = s % 2, (s + 1) % 2
        for m in range(2):
            for i in range(2):
                w[m, now, s + depth + i, rows, :] = state[s, 2 * upper[m] + i]
        for i in range(depth):
            for m in range(2):
                r = s + 1 + i
                core, beside = neighbours(w, (m, now), r, edge_low, edge_high, nx)
                fresh = keep * core + spread * beside
                if r == 1:
                    fresh = came[m][depth] * fresh
                else:
                    fresh = half_of(m, r, kinds[s]) * fresh
                if r >= depth:
                    at = place(m, r)
                    product = fresh * margin[s, upper[m] * depth + r - depth].astype(jnp.float32)
                    edge_dens[upper[m] * depth + r - depth, kinds[s]] += product
                    total[...] += folded(product)
                    if s == rest:
                        final[at] = fresh.astype(jnp.bfloat16)
                elif m == 0:
                    fresh = inside * fresh
                if s < rest:
                    if r > 1:
                        fresh = half_of(m, r, kinds[s + 1]) * fresh
                    w[m, later, r, rows, :] = fresh
        if s == 0:
            part = jnp.sum(inner_sums[0] + total[...], axis=0, keepdims=True)
    whole = jnp.sum(inner_sums[1] + total[...], axis=0, keepdims=True)
    both = jnp.concatenate([part, whole], 0)
    sums[...] = jnp.broadcast_to(both[None], sums.shape)
    for p in range(planes - 2 * depth):
        final[depth + p] = middle[p]


def weigh_kernel(cells, params, sums, dens, edge_dens, out, extra):
    planes, _, nx, ny = dens.shape
    depth = edge_dens.shape[0] // 2
    both = jnp.sum(sums[...], axis=0)
    partition = jnp.sum(both[0:1]) / cells
    weight = params[1:2] / splat(partition)
    first_row = lax.broadcasted_iota(jnp.int32, extra.shape, 0) == 0
    extra[...] = jnp.where(first_row, weight * both[1:2], 0.0)

    def body(p, carry):
        for t in range(2):
            out[p, t * nx : (t + 1) * nx, :] = weight * dens[p, t]
        return carry

    lax.fori_loop(depth, planes - depth, body, 0, unroll=True)

    def ends(p, carry):
        for t in range(2):
            out[p, t * nx : (t + 1) * nx, :] = weight * edge_dens[p, t]
            out[planes - 1 - p, t * nx : (t + 1) * nx, :] = weight * edge_dens[depth + p, t]
        return carry

    lax.fori_loop(0, depth, ends, 0, unroll=True)


def reduce_kernel(arrived, extra, out):
    acc = arrived[0]
    for c in range(1, arrived.shape[0]):
        acc = acc + arrived[c]
    out[0 : acc.shape[0]] = acc
    out[acc.shape[0] :] = extra[...]


def spread_kernel(pair, blocks):
    both = pair[0] + pair[1]
    blocks[...] = jnp.broadcast_to(both[None], blocks.shape)


def update_kernel(cells, blocks, fields, out):
    _, planes, nx, ny = fields.shape
    level = splat(jnp.sum(jnp.sum(blocks[:, 2 * nx :], axis=0)) / cells)

    def body(p, carry):
        first, second = blocks[p, 0:nx, :], blocks[p, nx : 2 * nx, :]
        pressure = stiffness * (first + second - level)
        old = fields[0, p]
        out[0, p] = old + mixing * (flory_chi * second + pressure - old)
        old = fields[1, p]
        out[1, p] = old + mixing * (flory_chi * first + pressure - old)
        return carry

    lax.fori_loop(0, planes, body, 0, unroll=2)


def call(kernel, outs, scratch, args, smem, flops, name, vmem=2, hbm=0, kinds=False):
    size = sum(a.size * a.dtype.itemsize for a in args) + sum(
        o.size * o.dtype.itemsize for o in outs
    )
    anywhere = pl.BlockSpec(memory_space=pltpu.HBM)
    return pl.pallas_call(
        kernel,
        out_shape=outs,
        in_specs=[SMEM] * smem + [VMEM] * (len(args) - smem - hbm) + [anywhere] * hbm,
        out_specs=[VMEM] * (len(outs) - kinds) + [SMEM] * kinds,
        scratch_shapes=scratch,
        compiler_params=pltpu.CompilerParams(vmem_limit_bytes=vmem * 2**20),
        cost_estimate=pl.CostEstimate(flops=flops, bytes_accessed=size, transcendentals=0),
        name=name,
    )(*args)


def in_hbm(x):
    return pltpu.with_memory_space_constraint(x, pltpu.HBM)


def f32(*shape):
    return jax.ShapeDtypeStruct(shape, jnp.float32)


def body(q_init, q_back, fields, lengths, counts, types):
    _, planes, nx, ny = q_init.shape
    depth = q_back.shape[1]
    cells = float(lax.axis_size(SLAB) * planes * nx * ny)
    q, back = q_init[0], q_back[0]
    types = types.T
    peers = lax.axis_size(XY)
    slabs = lax.axis_size(SLAB)
    message = f32(3 * depth - 3, nx, ny)
    classes = lengths.shape[0]

    outward, inward, params, kinds = call(
        edges_kernel,
        [message, message, f32(8, ny), jax.ShapeDtypeStruct((depth,), jnp.int32)],
        [
            pltpu.VMEM((2, depth, nx, ny), jnp.bfloat16),
            pltpu.VMEM((2, 4, nx, ny), jnp.float32),
            pltpu.SMEM((classes,), jnp.int32),
            pltpu.SMEM((classes,), jnp.int32),
            pltpu.SMEM((depth, classes), jnp.int32),
            pltpu.SemaphoreType.DMA((6 * depth + 3,)),
        ],
        tuple(map(in_hbm, (lengths, counts, types, q, fields))),
        0,
        10**6,
        "edges",
        vmem=4,
        hbm=5,
        kinds=True,
    )
    across = [(i, i + 1) for i in range(1, slabs - 1, 2)]
    within = [(i, i + 1) for i in range(0, slabs, 2)]
    outer = lax.ppermute(outward, SLAB, across + [(b, a) for a, b in across])
    near = lax.ppermute(inward, SLAB, within + [(b, a) for a, b in within])

    padded = nx + 2 * TOP
    half, state, dens, middle, sums, margin = call(
        inner_kernel,
        [
            f32(2, planes, nx, ny),
            f32(depth, 4, nx, ny),
            f32(planes, 2, nx, ny),
            jax.ShapeDtypeStruct((planes - 2 * depth, nx, ny), jnp.bfloat16),
            f32(2, 8, ny),
            jax.ShapeDtypeStruct((depth, 2 * depth, nx, ny), back.dtype),
        ],
        [
            pltpu.VMEM((2, planes, padded, ny), jnp.float32),
            pltpu.VMEM((8, ny), jnp.float32),
            pltpu.VMEM(back.shape, back.dtype),
            pltpu.SemaphoreType.DMA((depth,)),
        ],
        (kinds, params, q, fields, in_hbm(back)),
        1,
        10**8,
        "inner",
        vmem=8,
        hbm=1,
    )
    final, edge_dens, sums = call(
        outer_kernel,
        [
            jax.ShapeDtypeStruct((planes, nx, ny), jnp.bfloat16),
            f32(2 * depth, 2, nx, ny),
            f32(slabs, 2, ny),
        ],
        [
            pltpu.VMEM((2, 2, 2 * depth + 2, padded, ny), jnp.float32),
            pltpu.VMEM((8, ny), jnp.float32),
        ],
        (kinds, params, outer, near, half, state, dens, middle, sums, margin),
        1,
        10**8,
        "outer",
        vmem=8,
    )
    sums = lax.all_to_all(sums, SLAB, 0, 0, tiled=True)
    sent, extra = call(
        functools.partial(weigh_kernel, cells),
        [f32(peers, 2 * nx, ny), f32(8, ny)],
        [],
        (params, sums, dens, edge_dens),
        0,
        10**6,
        "weigh",
        vmem=8,
    )
    arrived = lax.all_to_all(sent, XY, 0, 0, tiled=True)
    (own,) = call(
        reduce_kernel, [f32(2 * nx + 8, ny)], [], (arrived, extra), 0, 10**6, "reduce", vmem=8
    )
    pair = lax.all_gather(own, "zh", axis=0, tiled=False)
    (blocks,) = call(
        spread_kernel, [f32(peers, 2 * nx + 8, ny)], [], (pair,), 0, 10**6, "spread", vmem=8
    )
    blocks = lax.all_to_all(blocks, XY, 0, 0, tiled=True)
    (fields_new,) = call(
        functools.partial(update_kernel, cells),
        [f32(2, planes, nx, ny)],
        [],
        (blocks, fields),
        0,
        10**6,
        "update",
        vmem=8,
    )
    return fields_new, final[None]


def solution(mesh):
    finer = Mesh(mesh.devices.reshape(2, 4, 4, mesh.shape["slab"]), ("zh", "y", "x", SLAB))
    in_specs = (
        P(CLS, SLAB, None, None),
        P(CLS, None, SLAB, None, None),
        P(None, SLAB, None, None),
        P(),
        P(),
        P(),
    )
    out_specs = (P(None, SLAB, None, None), P(CLS, SLAB, None, None))
    return jax.shard_map(body, mesh=finer, in_specs=in_specs, out_specs=out_specs, check_vma=False)
```

```python
import functools

import jax
import jax.numpy as jnp
from jax import lax
from jax.experimental import pallas as pl
from jax.experimental.pallas import tpu as pltpu
from jax.sharding import Mesh
from jax.sharding import PartitionSpec as P

CLS = ("zh", "y", "x")
XY = ("y", "x")
SLAB = "slab"

flory_chi = 2.0
stiffness = 1.0
mixing = 0.5
diffusion_scale = 0.125

VMEM = pl.BlockSpec(memory_space=pltpu.VMEM)
SMEM = pl.BlockSpec(memory_space=pltpu.SMEM)
UNROLL = True
TOP = 8


def own_class():
    return (lax.axis_index("zh") * 4 + lax.axis_index("y")) * 4 + lax.axis_index("x")


def splat(value, shape=(1, 128)):
    return jnp.full(shape, value, jnp.float32)


def folded(plane):
    return jnp.sum(plane.reshape(-1, 8, plane.shape[-1]), axis=0)


def neighbours(w, at, p, lane_low, lane_high, nx):
    core = w[(*at, p, slice(TOP, TOP + nx))]
    total = w[(*at, p - 1, slice(TOP, TOP + nx))] + w[(*at, p + 1, slice(TOP, TOP + nx))]
    total = total + w[(*at, p, slice(TOP - 1, TOP + nx - 1))]
    total = total + w[(*at, p, slice(TOP + 1, TOP + nx + 1))]
    ny = core.shape[-1]
    before = jnp.where(lane_low, 0.0, pltpu.roll(core, 1, 1))
    after = jnp.where(lane_high, 0.0, pltpu.roll(core, ny - 1, 1))
    return core, total + before + after


def lane_edges(nx, ny):
    lane = lax.broadcasted_iota(jnp.int32, (nx, ny), 1)
    return lane == 0, lane == ny - 1


def clear_margins(w, nx):
    blank = jnp.zeros(w.shape[:2] + (TOP, w.shape[-1]), jnp.float32)
    w[:, :, 0:TOP, :] = blank
    w[:, :, TOP + nx : TOP + nx + TOP, :] = blank


def sides():
    core = lax.rem(lax.axis_index(SLAB), 2)
    return core, 1 - core


def edges_kernel(
    lengths,
    counts,
    types,
    q,
    fields,
    outward,
    inward,
    params,
    kinds,
    ends,
    raw,
    own_lengths,
    own_counts,
    own_types,
    sems,
):
    planes = q.shape[0]
    depth = types.shape[0]
    cls = own_class()
    messages = (outward, inward)
    copies = [(lengths, own_lengths), (counts, own_counts), (types, own_types)]
    for m, upper in enumerate(sides()):
        start, turn = upper * (planes - depth) + (1 - upper) * (depth - 1), 2 * upper - 1
        for r in range(depth):
            at = start + turn * r
            copies.append((q.at[at], ends.at[m, r]))
            for t in range(2):
                to = raw.at[m, 2 * r + t] if r < 2 else messages[m].at[depth + 1 + 2 * (r - 2) + t]
                copies.append((fields.at[t, at], to))
    copies = [pltpu.make_async_copy(a, b, sems.at[i]) for i, (a, b) in enumerate(copies)]
    for copy in copies:
        copy.start()
    for copy in copies[:3]:
        copy.wait()
    whole = own_lengths[0]
    for c in range(1, own_lengths.shape[0]):
        whole = whole + own_lengths[c]
    length = splat(own_lengths[cls].astype(jnp.float32))
    size = length / splat(own_counts[cls].astype(jnp.float32))
    fraction = length / splat(whole.astype(jnp.float32))
    params[0:1] = size
    params[1:2] = fraction * size
    for s in range(depth):
        kinds[s] = own_types[s, cls]
    first, second = own_types[0, cls], own_types[1, cls]
    scale = -0.5 * size
    for copy in copies[3:]:
        copy.wait()
    for m, message in enumerate(messages):
        for r in range(depth):
            chosen = raw[m, 2 * r + first] if r < 2 else message[depth + 1 + 2 * (r - 2) + first]
            message[r] = jnp.exp(scale * chosen) * ends[m, r].astype(jnp.float32)
        message[depth] = jnp.exp(scale * (raw[m, 2 + first] + raw[m, 2 + second]))


def inner_kernel(
    kinds, params, q, fields, source, half, state, dens, middle, sums, margin, w, total, back, sems
):
    planes, nx, ny = q.shape
    depth = back.shape[0]
    copies = [pltpu.make_async_copy(source.at[s], back.at[s], sems.at[s]) for s in range(depth)]
    for copy in copies:
        copy.start()
    size = params[0:1]
    spread = diffusion_scale * size
    keep = 1.0 - 6.0 * spread
    scale = -0.5 * size
    kinds = [kinds[s] for s in range(depth)]
    edge_low, edge_high = lane_edges(nx, ny)
    clear_margins(w, nx)
    total[...] = jnp.zeros_like(total)
    rows = slice(TOP, TOP + nx)

    def first(p, carry):
        half[0, p] = jnp.exp(scale * fields[0, p])
        half[1, p] = jnp.exp(scale * fields[1, p])
        w[0, p, rows, :] = half[kinds[0], p] * q[p].astype(jnp.float32)
        dens[p, 0] = jnp.zeros((nx, ny), jnp.float32)
        dens[p, 1] = jnp.zeros((nx, ny), jnp.float32)
        return carry

    lax.fori_loop(0, planes, first, 0, unroll=2)

    for s in range(depth):
        now, later = s % 2, (s + 1) % 2
        kind = kinds[s]
        last = s == depth - 1
        copies[s].wait()
        for i, p in enumerate((s, s + 1, planes - 1 - s, planes - 2 - s)):
            state[s, i] = w[now, p, rows, :]

        def each(p, carry):
            core, beside = neighbours(w, (now,), p, edge_low, edge_high, nx)
            fresh = half[kind, p] * (keep * core + spread * beside)
            product = fresh * back[s, p].astype(jnp.float32)
            dens[p, kind] += product
            total[...] += folded(product)
            if last:
                middle[p - depth] = fresh.astype(jnp.bfloat16)
            else:
                w[later, p, rows, :] = half[kinds[s + 1], p] * fresh
            return carry

        lax.fori_loop(s + 1, planes - 1 - s, each, 0, unroll=UNROLL)
        if s == 0:
            sums[0] = total[...]
        for p in range(depth):
            margin[s, p] = back[s, p]
            margin[s, depth + p] = back[s, planes - 1 - p]
    sums[1] = total[...]


def outer_kernel(
    kinds,
    params,
    outer,
    near,
    half,
    state,
    dens,
    middle,
    inner_sums,
    margin,
    final,
    edge_dens,
    sums,
    w,
    total,
    last,
    sems,
):
    planes, nx, ny = final.shape
    kept = middle.shape[0]
    copies = [
        pltpu.make_async_copy(
            middle, final.at[pl.ds((planes - kept) // 2, kept)], sems.at[2]
        )
    ]
    copies[0].start()
    depth = margin.shape[0]
    slab = lax.axis_index(SLAB)
    inside = jnp.logical_and(slab > 0, slab < lax.axis_size(SLAB) - 1)
    inside = splat(jnp.where(inside, 1.0, 0.0))
    size = params[0:1]
    spread = diffusion_scale * size
    keep = 1.0 - 6.0 * spread
    scale = -0.5 * size
    kinds = [kinds[s] for s in range(depth)]
    edge_low, edge_high = lane_edges(nx, ny)
    for side in range(2):
        clear_margins(w.at[side], nx)
    total[...] = jnp.zeros_like(total)
    rows = slice(TOP, TOP + nx)
    came = (outer, near)
    rest = depth - 1
    upper = sides()

    def place(m, r):
        return upper[m] * (planes - 1) + (1 - 2 * upper[m]) * (r - depth)

    def half_of(m, r, kind):
        if r >= depth:
            return half[kind, place(m, r)]
        return jnp.exp(scale * came[m][depth + 1 + 2 * (r - 2) + kind])

    for m in range(2):
        for r in range(depth):
            w[m, 0, r, rows, :] = came[m][r]
        for p in range(depth):
            for t in range(2):
                edge_dens[upper[m] * depth + p, t] = dens[place(m, depth + p), t]

    for s in range(depth):
        now, later = s % 2, (s + 1) % 2
        for m in range(2):
            for i in range(2):
                w[m, now, s + depth + i, rows, :] = state[s, 2 * upper[m] + i]
        for i in range(depth):
            for m in range(2):
                r = s + 1 + i
                core, beside = neighbours(w, (m, now), r, edge_low, edge_high, nx)
                fresh = keep * core + spread * beside
                if r == 1:
                    fresh = came[m][depth] * fresh
                else:
                    fresh = half_of(m, r, kinds[s]) * fresh
                if r >= depth:
                    at = place(m, r)
                    product = fresh * margin[s, upper[m] * depth + r - depth].astype(jnp.float32)
                    edge_dens[upper[m] * depth + r - depth, kinds[s]] += product
                    total[...] += folded(product)
                    if s == rest:
                        last[upper[m] * depth + at - upper[m] * (planes - depth)] = fresh.astype(
                            jnp.bfloat16
                        )
                elif m == 0:
                    fresh = inside * fresh
                if s < rest:
                    if r > 1:
                        fresh = half_of(m, r, kinds[s + 1]) * fresh
                    w[m, later, r, rows, :] = fresh
        if s == 0:
            part = jnp.sum(inner_sums[0] + total[...], axis=0, keepdims=True)
    for side in range(2):
        to = final.at[pl.ds(side * (planes - depth), depth)]
        copy = pltpu.make_async_copy(last.at[pl.ds(side * depth, depth)], to, sems.at[side])
        copy.start()
        copies.append(copy)
    whole = jnp.sum(inner_sums[1] + total[...], axis=0, keepdims=True)
    both = jnp.concatenate([part, whole], 0)
    sums[...] = jnp.broadcast_to(both[None], sums.shape)
    for copy in copies:
        copy.wait()


def weigh_kernel(cells, params, sums, dens, edge_dens, out):
    planes, _, nx, ny = dens.shape
    depth = edge_dens.shape[0] // 2
    both = jnp.sum(sums[...], axis=0)
    partition = jnp.sum(both[0:1]) / cells
    weight = params[1:2] / splat(partition)
    level = weight * (jnp.sum(both[1:2]) / cells)
    shift = level * (stiffness / (flory_chi + 2.0 * stiffness))

    for p in range(planes):
        for t in range(2):
            if p < depth:
                mine = edge_dens[p, t]
            elif p >= planes - depth:
                mine = edge_dens[depth + planes - 1 - p, t]
            else:
                mine = dens[p, t]
            out[p, t * nx : (t + 1) * nx, :] = weight * mine - shift


def reduce_kernel(arrived, out):
    acc = arrived[0]
    for c in range(1, arrived.shape[0]):
        acc = acc + arrived[c]
    out[...] = acc


def spread_kernel(pair, blocks):
    both = pair[0] + pair[1]
    blocks[...] = jnp.broadcast_to(both[None], blocks.shape)


def update_kernel(blocks, fields, out, fresh, sems):
    _, planes, nx, ny = fields.shape
    chunk = planes // sems.shape[0]
    copies = []
    for i in range(sems.shape[0]):
        for p in range(i * chunk, (i + 1) * chunk):
            first, second = blocks[p, 0:nx, :], blocks[p, nx : 2 * nx, :]
            pressure = stiffness * (first + second)
            old = fields[0, p]
            fresh[0, p] = old + mixing * (flory_chi * second + pressure - old)
            old = fields[1, p]
            fresh[1, p] = old + mixing * (flory_chi * first + pressure - old)
        at = pl.ds(i * chunk, chunk)
        for t in range(2):
            copy = pltpu.make_async_copy(fresh.at[t, at], out.at[t, at], sems.at[i, t])
            copy.start()
            copies.append(copy)
    for copy in copies:
        copy.wait()


def call(kernel, outs, scratch, args, smem, flops, name, vmem=2, hbm=0, kinds=False, far=()):
    size = sum(a.size * a.dtype.itemsize for a in args) + sum(
        o.size * o.dtype.itemsize for o in outs
    )
    anywhere = pl.BlockSpec(memory_space=pltpu.HBM)
    return pl.pallas_call(
        kernel,
        out_shape=outs,
        in_specs=[SMEM] * smem + [VMEM] * (len(args) - smem - hbm) + [anywhere] * hbm,
        out_specs=[anywhere if i in far else VMEM for i in range(len(outs) - kinds)]
        + [SMEM] * kinds,
        scratch_shapes=scratch,
        compiler_params=pltpu.CompilerParams(vmem_limit_bytes=vmem * 2**20),
        cost_estimate=pl.CostEstimate(flops=flops, bytes_accessed=size, transcendentals=0),
        name=name,
    )(*args)


def in_hbm(x):
    return pltpu.with_memory_space_constraint(x, pltpu.HBM)


def f32(*shape):
    return jax.ShapeDtypeStruct(shape, jnp.float32)


def body(q_init, q_back, fields, lengths, counts, types):
    _, planes, nx, ny = q_init.shape
    depth = q_back.shape[1]
    cells = float(lax.axis_size(SLAB) * planes * nx * ny)
    q, back = q_init[0], q_back[0]
    types = types.T
    peers = lax.axis_size(XY)
    slabs = lax.axis_size(SLAB)
    message = f32(3 * depth - 3, nx, ny)
    classes = lengths.shape[0]

    outward, inward, params, kinds = call(
        edges_kernel,
        [message, message, f32(8, ny), jax.ShapeDtypeStruct((depth,), jnp.int32)],
        [
            pltpu.VMEM((2, depth, nx, ny), jnp.bfloat16),
            pltpu.VMEM((2, 4, nx, ny), jnp.float32),
            pltpu.SMEM((classes,), jnp.int32),
            pltpu.SMEM((classes,), jnp.int32),
            pltpu.SMEM((depth, classes), jnp.int32),
            pltpu.SemaphoreType.DMA((6 * depth + 3,)),
        ],
        tuple(map(in_hbm, (lengths, counts, types, q, fields))),
        0,
        10**6,
        "edges",
        vmem=4,
        hbm=5,
        kinds=True,
    )
    across = [(i, i + 1) for i in range(1, slabs - 1, 2)]
    within = [(i, i + 1) for i in range(0, slabs, 2)]
    outer = lax.ppermute(outward, SLAB, across + [(b, a) for a, b in across])
    near = lax.ppermute(inward, SLAB, within + [(b, a) for a, b in within])

    padded = nx + 2 * TOP
    half, state, dens, middle, sums, margin = call(
        inner_kernel,
        [
            f32(2, planes, nx, ny),
            f32(depth, 4, nx, ny),
            f32(planes, 2, nx, ny),
            jax.ShapeDtypeStruct((planes - 2 * depth, nx, ny), jnp.bfloat16),
            f32(2, 8, ny),
            jax.ShapeDtypeStruct((depth, 2 * depth, nx, ny), back.dtype),
        ],
        [
            pltpu.VMEM((2, planes, padded, ny), jnp.float32),
            pltpu.VMEM((8, ny), jnp.float32),
            pltpu.VMEM(back.shape, back.dtype),
            pltpu.SemaphoreType.DMA((depth,)),
        ],
        (kinds, params, q, fields, in_hbm(back)),
        1,
        10**8,
        "inner",
        vmem=8,
        hbm=1,
    )
    final, edge_dens, sums = call(
        outer_kernel,
        [
            jax.ShapeDtypeStruct((planes, nx, ny), jnp.bfloat16),
            f32(2 * depth, 2, nx, ny),
            f32(slabs, 2, ny),
        ],
        [
            pltpu.VMEM((2, 2, 2 * depth + 2, padded, ny), jnp.float32),
            pltpu.VMEM((8, ny), jnp.float32),
            pltpu.VMEM((2 * depth, nx, ny), jnp.bfloat16),
            pltpu.SemaphoreType.DMA((3,)),
        ],
        (kinds, params, outer, near, half, state, dens, middle, sums, margin),
        1,
        10**8,
        "outer",
        vmem=8,
        far=(0,),
    )
    sums = lax.all_to_all(sums, SLAB, 0, 0, tiled=True)
    (sent,) = call(
        functools.partial(weigh_kernel, cells),
        [f32(peers, 2 * nx, ny)],
        [],
        (params, sums, dens, edge_dens),
        0,
        10**6,
        "weigh",
        vmem=8,
    )
    arrived = lax.all_to_all(sent, XY, 0, 0, tiled=True)
    (own,) = call(reduce_kernel, [f32(2 * nx, ny)], [], (arrived,), 0, 10**6, "reduce", vmem=8)
    pair = lax.all_gather(own, "zh", axis=0, tiled=False)
    (blocks,) = call(
        spread_kernel, [f32(peers, 2 * nx, ny)], [], (pair,), 0, 10**6, "spread", vmem=8
    )
    blocks = lax.all_to_all(blocks, XY, 0, 0, tiled=True)
    (fields_new,) = call(
        update_kernel,
        [f32(2, planes, nx, ny)],
        [
            pltpu.VMEM((2, planes, nx, ny), jnp.float32),
            pltpu.SemaphoreType.DMA((4, 2)),
        ],
        (blocks, fields),
        0,
        10**6,
        "update",
        vmem=8,
        far=(0,),
    )
    return fields_new, final[None]


def solution(mesh):
    finer = Mesh(mesh.devices.reshape(2, 4, 4, mesh.shape["slab"]), ("zh", "y", "x", SLAB))
    in_specs = (
        P(CLS, SLAB, None, None),
        P(CLS, None, SLAB, None, None),
        P(None, SLAB, None, None),
        P(),
        P(),
        P(),
    )
    out_specs = (P(None, SLAB, None, None), P(CLS, SLAB, None, None))
    return jax.shard_map(body, mesh=finer, in_specs=in_specs, out_specs=out_specs, check_vma=False)
```

```python
import functools

import jax
import jax.numpy as jnp
from jax import lax
from jax.experimental import pallas as pl
from jax.experimental.pallas import tpu as pltpu
from jax.sharding import Mesh
from jax.sharding import PartitionSpec as P

CLS = ("zh", "y", "x")
XY = ("y", "x")
SLAB = "slab"

flory_chi = 2.0
stiffness = 1.0
mixing = 0.5
diffusion_scale = 0.125

VMEM = pl.BlockSpec(memory_space=pltpu.VMEM)
SMEM = pl.BlockSpec(memory_space=pltpu.SMEM)
UNROLL = True
TOP = 8


def own_class():
    return (lax.axis_index("zh") * 4 + lax.axis_index("y")) * 4 + lax.axis_index("x")


def splat(value, shape=(1, 128)):
    return jnp.full(shape, value, jnp.float32)


def folded(plane):
    return jnp.sum(plane.reshape(-1, 8, plane.shape[-1]), axis=0)


def neighbours(w, at, p, lane_low, lane_high, nx):
    core = w[(*at, p, slice(TOP, TOP + nx))]
    total = w[(*at, p - 1, slice(TOP, TOP + nx))] + w[(*at, p + 1, slice(TOP, TOP + nx))]
    total = total + w[(*at, p, slice(TOP - 1, TOP + nx - 1))]
    total = total + w[(*at, p, slice(TOP + 1, TOP + nx + 1))]
    ny = core.shape[-1]
    before = jnp.where(lane_low, 0.0, pltpu.roll(core, 1, 1))
    after = jnp.where(lane_high, 0.0, pltpu.roll(core, ny - 1, 1))
    return core, total + before + after


def lane_edges(nx, ny):
    lane = lax.broadcasted_iota(jnp.int32, (nx, ny), 1)
    return lane == 0, lane == ny - 1


def clear_margins(w, nx):
    blank = jnp.zeros(w.shape[:2] + (TOP, w.shape[-1]), jnp.float32)
    w[:, :, 0:TOP, :] = blank
    w[:, :, TOP + nx : TOP + nx + TOP, :] = blank


def sides():
    core = lax.rem(lax.axis_index(SLAB), 2)
    return core, 1 - core


def edges_kernel(
    lengths,
    counts,
    types,
    q,
    fields,
    outward,
    inward,
    params,
    kinds,
    ends,
    raw,
    own_lengths,
    own_counts,
    own_types,
    sems,
):
    planes = q.shape[0]
    depth = types.shape[0]
    cls = own_class()
    messages = (outward, inward)
    copies = [(lengths, own_lengths), (counts, own_counts), (types, own_types)]
    for m, upper in enumerate(sides()):
        start, turn = upper * (planes - depth) + (1 - upper) * (depth - 1), 2 * upper - 1
        for r in range(depth):
            at = start + turn * r
            copies.append((q.at[at], ends.at[m, r]))
            for t in range(2):
                to = raw.at[m, 2 * r + t] if r < 2 else messages[m].at[depth + 1 + 2 * (r - 2) + t]
                copies.append((fields.at[t, at], to))
    copies = [pltpu.make_async_copy(a, b, sems.at[i]) for i, (a, b) in enumerate(copies)]
    for copy in copies:
        copy.start()
    for copy in copies[:3]:
        copy.wait()
    whole = own_lengths[0]
    for c in range(1, own_lengths.shape[0]):
        whole = whole + own_lengths[c]
    length = splat(own_lengths[cls].astype(jnp.float32))
    size = length / splat(own_counts[cls].astype(jnp.float32))
    fraction = length / splat(whole.astype(jnp.float32))
    params[0:1] = size
    params[1:2] = fraction * size
    for s in range(depth):
        kinds[s] = own_types[s, cls]
    first, second = own_types[0, cls], own_types[1, cls]
    scale = -0.5 * size
    for copy in copies[3:]:
        copy.wait()
    for m, message in enumerate(messages):
        for r in range(depth):
            chosen = raw[m, 2 * r + first] if r < 2 else message[depth + 1 + 2 * (r - 2) + first]
            message[r] = jnp.exp(scale * chosen) * ends[m, r].astype(jnp.float32)
        message[depth] = jnp.exp(scale * (raw[m, 2 + first] + raw[m, 2 + second]))


def inner_kernel(
    kinds, params, q, fields, source, half, state, dens, middle, sums, margin, w, total, back, sems
):
    planes, nx, ny = q.shape
    depth = back.shape[0]
    copies = [pltpu.make_async_copy(source.at[s], back.at[s], sems.at[s]) for s in range(depth)]
    for copy in copies:
        copy.start()
    size = params[0:1]
    spread = diffusion_scale * size
    keep = 1.0 - 6.0 * spread
    scale = -0.5 * size
    kinds = [kinds[s] for s in range(depth)]
    edge_low, edge_high = lane_edges(nx, ny)
    clear_margins(w, nx)
    total[...] = jnp.zeros_like(total)
    rows = slice(TOP, TOP + nx)

    def first(p, carry):
        half[0, p] = jnp.exp(scale * fields[0, p])
        half[1, p] = jnp.exp(scale * fields[1, p])
        w[0, p, rows, :] = half[kinds[0], p] * q[p].astype(jnp.float32)
        dens[p, 0] = jnp.zeros((nx, ny), jnp.float32)
        dens[p, 1] = jnp.zeros((nx, ny), jnp.float32)
        return carry

    lax.fori_loop(0, planes, first, 0, unroll=2)

    for s in range(depth):
        now, later = s % 2, (s + 1) % 2
        kind = kinds[s]
        last = s == depth - 1
        copies[s].wait()
        for i, p in enumerate((s, s + 1, planes - 1 - s, planes - 2 - s)):
            state[s, i] = w[now, p, rows, :]

        def each(p, carry):
            core, beside = neighbours(w, (now,), p, edge_low, edge_high, nx)
            fresh = half[kind, p] * (keep * core + spread * beside)
            product = fresh * back[s, p].astype(jnp.float32)
            dens[p, kind] += product
            total[...] += folded(product)
            if last:
                middle[p - depth] = fresh.astype(jnp.bfloat16)
            else:
                w[later, p, rows, :] = half[kinds[s + 1], p] * fresh
            return carry

        lax.fori_loop(s + 1, planes - 1 - s, each, 0, unroll=UNROLL)
        if s == 0:
            sums[0] = total[...]
        for p in range(depth):
            margin[s, p] = back[s, p]
            margin[s, depth + p] = back[s, planes - 1 - p]
    sums[1] = total[...]


def outer_kernel(
    kinds,
    params,
    outer,
    near,
    half,
    state,
    dens,
    inner_sums,
    margin,
    last,
    edge_dens,
    sums,
    w,
    total,
):
    _, planes, nx, ny = half.shape
    depth = margin.shape[0]
    slab = lax.axis_index(SLAB)
    inside = jnp.logical_and(slab > 0, slab < lax.axis_size(SLAB) - 1)
    inside = splat(jnp.where(inside, 1.0, 0.0))
    size = params[0:1]
    spread = diffusion_scale * size
    keep = 1.0 - 6.0 * spread
    scale = -0.5 * size
    kinds = [kinds[s] for s in range(depth)]
    edge_low, edge_high = lane_edges(nx, ny)
    for side in range(2):
        clear_margins(w.at[side], nx)
    total[...] = jnp.zeros_like(total)
    rows = slice(TOP, TOP + nx)
    came = (outer, near)
    rest = depth - 1
    upper = sides()

    def place(m, r):
        return upper[m] * (planes - 1) + (1 - 2 * upper[m]) * (r - depth)

    def half_of(m, r, kind):
        if r >= depth:
            return half[kind, place(m, r)]
        return jnp.exp(scale * came[m][depth + 1 + 2 * (r - 2) + kind])

    for m in range(2):
        for r in range(depth):
            w[m, 0, r, rows, :] = came[m][r]
        for p in range(depth):
            for t in range(2):
                edge_dens[upper[m] * depth + p, t] = dens[place(m, depth + p), t]

    for s in range(depth):
        now, later = s % 2, (s + 1) % 2
        for m in range(2):
            for i in range(2):
                w[m, now, s + depth + i, rows, :] = state[s, 2 * upper[m] + i]
        for i in range(depth):
            for m in range(2):
                r = s + 1 + i
                core, beside = neighbours(w, (m, now), r, edge_low, edge_high, nx)
                fresh = keep * core + spread * beside
                if r == 1:
                    fresh = came[m][depth] * fresh
                else:
                    fresh = half_of(m, r, kinds[s]) * fresh
                if r >= depth:
                    at = place(m, r)
                    product = fresh * margin[s, upper[m] * depth + r - depth].astype(jnp.float32)
                    edge_dens[upper[m] * depth + r - depth, kinds[s]] += product
                    total[...] += folded(product)
                    if s == rest:
                        last[upper[m] * depth + at - upper[m] * (planes - depth)] = fresh.astype(
                            jnp.bfloat16
                        )
                elif m == 0:
                    fresh = inside * fresh
                if s < rest:
                    if r > 1:
                        fresh = half_of(m, r, kinds[s + 1]) * fresh
                    w[m, later, r, rows, :] = fresh
        if s == 0:
            part = jnp.sum(inner_sums[0] + total[...], axis=0, keepdims=True)
    whole = jnp.sum(inner_sums[1] + total[...], axis=0, keepdims=True)
    both = jnp.concatenate([part, whole], 0)
    sums[...] = jnp.broadcast_to(both[None], sums.shape)


def weigh_kernel(cells, params, sums, dens, edge_dens, out):
    planes, _, nx, ny = dens.shape
    depth = edge_dens.shape[0] // 2
    both = jnp.sum(sums[...], axis=0)
    partition = jnp.sum(both[0:1]) / cells
    weight = params[1:2] / splat(partition)
    level = weight * (jnp.sum(both[1:2]) / cells)
    shift = level * (stiffness / (flory_chi + 2.0 * stiffness))

    for p in range(planes):
        for t in range(2):
            if p < depth:
                mine = edge_dens[p, t]
            elif p >= planes - depth:
                mine = edge_dens[depth + planes - 1 - p, t]
            else:
                mine = dens[p, t]
            out[p, t * nx : (t + 1) * nx, :] = weight * mine - shift


def reduce_kernel(arrived, out):
    acc = arrived[0]
    for c in range(1, arrived.shape[0]):
        acc = acc + arrived[c]
    out[...] = acc


def spread_kernel(pair, blocks):
    both = pair[0] + pair[1]
    blocks[...] = jnp.broadcast_to(both[None], blocks.shape)


def update_kernel(blocks, fields, middle, last, out, final, fresh, sems, end_sems):
    _, planes, nx, ny = fields.shape
    chunk = planes // sems.shape[0]
    depth = last.shape[0] // 2
    parts = (
        (middle, depth, middle.shape[0]),
        (last.at[pl.ds(0, depth)], 0, depth),
        (last.at[pl.ds(depth, depth)], planes - depth, depth),
    )
    copies = []
    for i, (part, at, count) in enumerate(parts):
        copies.append(pltpu.make_async_copy(part, final.at[pl.ds(at, count)], end_sems.at[i]))
        copies[-1].start()
    for i in range(sems.shape[0]):
        for p in range(i * chunk, (i + 1) * chunk):
            first, second = blocks[p, 0:nx, :], blocks[p, nx : 2 * nx, :]
            pressure = stiffness * (first + second)
            old = fields[0, p]
            fresh[0, p] = old + mixing * (flory_chi * second + pressure - old)
            old = fields[1, p]
            fresh[1, p] = old + mixing * (flory_chi * first + pressure - old)
        at = pl.ds(i * chunk, chunk)
        for t in range(2):
            copy = pltpu.make_async_copy(fresh.at[t, at], out.at[t, at], sems.at[i, t])
            copy.start()
            copies.append(copy)
    for copy in copies:
        copy.wait()


def call(kernel, outs, scratch, args, smem, flops, name, vmem=2, hbm=0, kinds=False, far=()):
    size = sum(a.size * a.dtype.itemsize for a in args) + sum(
        o.size * o.dtype.itemsize for o in outs
    )
    anywhere = pl.BlockSpec(memory_space=pltpu.HBM)
    return pl.pallas_call(
        kernel,
        out_shape=outs,
        in_specs=[SMEM] * smem + [VMEM] * (len(args) - smem - hbm) + [anywhere] * hbm,
        out_specs=[anywhere if i in far else VMEM for i in range(len(outs) - kinds)]
        + [SMEM] * kinds,
        scratch_shapes=scratch,
        compiler_params=pltpu.CompilerParams(vmem_limit_bytes=vmem * 2**20),
        cost_estimate=pl.CostEstimate(flops=flops, bytes_accessed=size, transcendentals=0),
        name=name,
    )(*args)


def in_hbm(x):
    return pltpu.with_memory_space_constraint(x, pltpu.HBM)


def f32(*shape):
    return jax.ShapeDtypeStruct(shape, jnp.float32)


def body(q_init, q_back, fields, lengths, counts, types):
    _, planes, nx, ny = q_init.shape
    depth = q_back.shape[1]
    cells = float(lax.axis_size(SLAB) * planes * nx * ny)
    q, back = q_init[0], q_back[0]
    types = types.T
    peers = lax.axis_size(XY)
    slabs = lax.axis_size(SLAB)
    message = f32(3 * depth - 3, nx, ny)
    classes = lengths.shape[0]

    outward, inward, params, kinds = call(
        edges_kernel,
        [message, message, f32(8, ny), jax.ShapeDtypeStruct((depth,), jnp.int32)],
        [
            pltpu.VMEM((2, depth, nx, ny), jnp.bfloat16),
            pltpu.VMEM((2, 4, nx, ny), jnp.float32),
            pltpu.SMEM((classes,), jnp.int32),
            pltpu.SMEM((classes,), jnp.int32),
            pltpu.SMEM((depth, classes), jnp.int32),
            pltpu.SemaphoreType.DMA((6 * depth + 3,)),
        ],
        tuple(map(in_hbm, (lengths, counts, types, q, fields))),
        0,
        10**6,
        "edges",
        vmem=4,
        hbm=5,
        kinds=True,
    )
    across = [(i, i + 1) for i in range(1, slabs - 1, 2)]
    within = [(i, i + 1) for i in range(0, slabs, 2)]
    outer = lax.ppermute(outward, SLAB, across + [(b, a) for a, b in across])
    near = lax.ppermute(inward, SLAB, within + [(b, a) for a, b in within])

    padded = nx + 2 * TOP
    half, state, dens, middle, sums, margin = call(
        inner_kernel,
        [
            f32(2, planes, nx, ny),
            f32(depth, 4, nx, ny),
            f32(planes, 2, nx, ny),
            jax.ShapeDtypeStruct((planes - 2 * depth, nx, ny), jnp.bfloat16),
            f32(2, 8, ny),
            jax.ShapeDtypeStruct((depth, 2 * depth, nx, ny), back.dtype),
        ],
        [
            pltpu.VMEM((2, planes, padded, ny), jnp.float32),
            pltpu.VMEM((8, ny), jnp.float32),
            pltpu.VMEM(back.shape, back.dtype),
            pltpu.SemaphoreType.DMA((depth,)),
        ],
        (kinds, params, q, fields, in_hbm(back)),
        1,
        10**8,
        "inner",
        vmem=8,
        hbm=1,
    )
    last, edge_dens, sums = call(
        outer_kernel,
        [
            jax.ShapeDtypeStruct((2 * depth, nx, ny), jnp.bfloat16),
            f32(2 * depth, 2, nx, ny),
            f32(slabs, 2, ny),
        ],
        [
            pltpu.VMEM((2, 2, 2 * depth + 2, padded, ny), jnp.float32),
            pltpu.VMEM((8, ny), jnp.float32),
        ],
        (kinds, params, outer, near, half, state, dens, sums, margin),
        1,
        10**8,
        "outer",
        vmem=8,
    )
    sums = lax.all_to_all(sums, SLAB, 0, 0, tiled=True)
    (sent,) = call(
        functools.partial(weigh_kernel, cells),
        [f32(peers, 2 * nx, ny)],
        [],
        (params, sums, dens, edge_dens),
        0,
        10**6,
        "weigh",
        vmem=8,
    )
    arrived = lax.all_to_all(sent, XY, 0, 0, tiled=True)
    (own,) = call(reduce_kernel, [f32(2 * nx, ny)], [], (arrived,), 0, 10**6, "reduce", vmem=8)
    pair = lax.all_gather(own, "zh", axis=0, tiled=False)
    (blocks,) = call(
        spread_kernel, [f32(peers, 2 * nx, ny)], [], (pair,), 0, 10**6, "spread", vmem=8
    )
    blocks = lax.all_to_all(blocks, XY, 0, 0, tiled=True)
    fields_new, final = call(
        update_kernel,
        [f32(2, planes, nx, ny), jax.ShapeDtypeStruct((planes, nx, ny), jnp.bfloat16)],
        [
            pltpu.VMEM((2, planes, nx, ny), jnp.float32),
            pltpu.SemaphoreType.DMA((4, 2)),
            pltpu.SemaphoreType.DMA((3,)),
        ],
        (blocks, fields, middle, last),
        0,
        10**6,
        "update",
        vmem=8,
        far=(0, 1),
    )
    return fields_new, final[None]


def solution(mesh):
    finer = Mesh(mesh.devices.reshape(2, 4, 4, mesh.shape["slab"]), ("zh", "y", "x", SLAB))
    in_specs = (
        P(CLS, SLAB, None, None),
        P(CLS, None, SLAB, None, None),
        P(None, SLAB, None, None),
        P(),
        P(),
        P(),
    )
    out_specs = (P(None, SLAB, None, None), P(CLS, SLAB, None, None))
    return jax.shard_map(body, mesh=finer, in_specs=in_specs, out_specs=out_specs, check_vma=False)
```

```python
import functools

import jax
import jax.numpy as jnp
from jax import lax
from jax.experimental import pallas as pl
from jax.experimental.pallas import tpu as pltpu
from jax.sharding import Mesh
from jax.sharding import PartitionSpec as P

CLS = ("zh", "y", "x")
XY = ("x", "y")
SLAB = "slab"

flory_chi = 2.0
stiffness = 1.0
mixing = 0.5
diffusion_scale = 0.125

VMEM = pl.BlockSpec(memory_space=pltpu.VMEM)
SMEM = pl.BlockSpec(memory_space=pltpu.SMEM)
UNROLL = True
TOP = 8


def own_class():
    return (lax.axis_index("zh") * 4 + lax.axis_index("y")) * 4 + lax.axis_index("x")


def splat(value, shape=(1, 128)):
    return jnp.full(shape, value, jnp.float32)


def folded(plane):
    return jnp.sum(plane.reshape(-1, 8, plane.shape[-1]), axis=0)


def neighbours(w, at, p, lane_low, lane_high, nx):
    core = w[(*at, p, slice(TOP, TOP + nx))]
    total = w[(*at, p - 1, slice(TOP, TOP + nx))] + w[(*at, p + 1, slice(TOP, TOP + nx))]
    total = total + w[(*at, p, slice(TOP - 1, TOP + nx - 1))]
    total = total + w[(*at, p, slice(TOP + 1, TOP + nx + 1))]
    ny = core.shape[-1]
    before = jnp.where(lane_low, 0.0, pltpu.roll(core, 1, 1))
    after = jnp.where(lane_high, 0.0, pltpu.roll(core, ny - 1, 1))
    return core, total + before + after


def lane_edges(nx, ny):
    lane = lax.broadcasted_iota(jnp.int32, (nx, ny), 1)
    return lane == 0, lane == ny - 1


def clear_margins(w, nx):
    blank = jnp.zeros(w.shape[:2] + (TOP, w.shape[-1]), jnp.float32)
    w[:, :, 0:TOP, :] = blank
    w[:, :, TOP + nx : TOP + nx + TOP, :] = blank


def sides():
    core = lax.rem(lax.axis_index(SLAB), 2)
    return core, 1 - core


def edges_kernel(
    lengths,
    counts,
    types,
    q,
    fields,
    outward,
    inward,
    params,
    kinds,
    ends,
    raw,
    own_lengths,
    own_counts,
    own_types,
    sems,
):
    planes = q.shape[0]
    depth = types.shape[0]
    cls = own_class()
    messages = (outward, inward)
    copies = [(lengths, own_lengths), (counts, own_counts), (types, own_types)]
    for m, upper in enumerate(sides()):
        start, turn = upper * (planes - depth) + (1 - upper) * (depth - 1), 2 * upper - 1
        for r in range(depth):
            at = start + turn * r
            copies.append((q.at[at], ends.at[m, r]))
            for t in range(2):
                to = raw.at[m, 2 * r + t] if r < 2 else messages[m].at[depth + 1 + 2 * (r - 2) + t]
                copies.append((fields.at[t, at], to))
    copies = [pltpu.make_async_copy(a, b, sems.at[i]) for i, (a, b) in enumerate(copies)]
    for copy in copies:
        copy.start()
    for copy in copies[:3]:
        copy.wait()
    whole = own_lengths[0]
    for c in range(1, own_lengths.shape[0]):
        whole = whole + own_lengths[c]
    length = splat(own_lengths[cls].astype(jnp.float32))
    size = length / splat(own_counts[cls].astype(jnp.float32))
    fraction = length / splat(whole.astype(jnp.float32))
    params[0:1] = size
    params[1:2] = fraction * size
    for s in range(depth):
        kinds[s] = own_types[s, cls]
    first, second = own_types[0, cls], own_types[1, cls]
    scale = -0.5 * size
    for copy in copies[3:]:
        copy.wait()
    for m, message in enumerate(messages):
        for r in range(depth):
            chosen = raw[m, 2 * r + first] if r < 2 else message[depth + 1 + 2 * (r - 2) + first]
            message[r] = jnp.exp(scale * chosen) * ends[m, r].astype(jnp.float32)
        message[depth] = jnp.exp(scale * (raw[m, 2 + first] + raw[m, 2 + second]))


def inner_kernel(
    kinds, params, q, fields, source, half, state, dens, middle, sums, margin, w, total, back, sems
):
    planes, nx, ny = q.shape
    depth = back.shape[0]
    copies = [pltpu.make_async_copy(source.at[s], back.at[s], sems.at[s]) for s in range(depth)]
    for copy in copies:
        copy.start()
    size = params[0:1]
    spread = diffusion_scale * size
    keep = 1.0 - 6.0 * spread
    scale = -0.5 * size
    kinds = [kinds[s] for s in range(depth)]
    edge_low, edge_high = lane_edges(nx, ny)
    clear_margins(w, nx)
    total[...] = jnp.zeros_like(total)
    rows = slice(TOP, TOP + nx)

    def first(p, carry):
        half[0, p] = jnp.exp(scale * fields[0, p])
        half[1, p] = jnp.exp(scale * fields[1, p])
        w[0, p, rows, :] = half[kinds[0], p] * q[p].astype(jnp.float32)
        dens[p, 0] = jnp.zeros((nx, ny), jnp.float32)
        dens[p, 1] = jnp.zeros((nx, ny), jnp.float32)
        return carry

    lax.fori_loop(0, planes, first, 0, unroll=2)

    for s in range(depth):
        now, later = s % 2, (s + 1) % 2
        kind = kinds[s]
        last = s == depth - 1
        copies[s].wait()
        for i, p in enumerate((s, s + 1, planes - 1 - s, planes - 2 - s)):
            state[s, i] = w[now, p, rows, :]

        def each(p, carry):
            core, beside = neighbours(w, (now,), p, edge_low, edge_high, nx)
            fresh = half[kind, p] * (keep * core + spread * beside)
            product = fresh * back[s, p].astype(jnp.float32)
            dens[p, kind] += product
            total[...] += folded(product)
            if last:
                middle[p - depth] = fresh.astype(jnp.bfloat16)
            else:
                w[later, p, rows, :] = half[kinds[s + 1], p] * fresh
            return carry

        lax.fori_loop(s + 1, planes - 1 - s, each, 0, unroll=UNROLL)
        if s == 0:
            sums[0] = total[...]
        for p in range(depth):
            margin[s, p] = back[s, p]
            margin[s, depth + p] = back[s, planes - 1 - p]
    sums[1] = total[...]


def outer_kernel(
    kinds,
    params,
    outer,
    near,
    half,
    state,
    dens,
    inner_sums,
    margin,
    last,
    edge_dens,
    sums,
    w,
    total,
):
    _, planes, nx, ny = half.shape
    depth = margin.shape[0]
    slab = lax.axis_index(SLAB)
    inside = jnp.logical_and(slab > 0, slab < lax.axis_size(SLAB) - 1)
    inside = splat(jnp.where(inside, 1.0, 0.0))
    size = params[0:1]
    spread = diffusion_scale * size
    keep = 1.0 - 6.0 * spread
    scale = -0.5 * size
    kinds = [kinds[s] for s in range(depth)]
    edge_low, edge_high = lane_edges(nx, ny)
    for side in range(2):
        clear_margins(w.at[side], nx)
    total[...] = jnp.zeros_like(total)
    rows = slice(TOP, TOP + nx)
    came = (outer, near)
    rest = depth - 1
    upper = sides()

    def place(m, r):
        return upper[m] * (planes - 1) + (1 - 2 * upper[m]) * (r - depth)

    def half_of(m, r, kind):
        if r >= depth:
            return half[kind, place(m, r)]
        return jnp.exp(scale * came[m][depth + 1 + 2 * (r - 2) + kind])

    for m in range(2):
        for r in range(depth):
            w[m, 0, r, rows, :] = came[m][r]
        for p in range(depth):
            for t in range(2):
                edge_dens[upper[m] * depth + p, t] = dens[place(m, depth + p), t]

    for s in range(depth):
        now, later = s % 2, (s + 1) % 2
        for m in range(2):
            for i in range(2):
                w[m, now, s + depth + i, rows, :] = state[s, 2 * upper[m] + i]
        for i in range(depth):
            for m in range(2):
                r = s + 1 + i
                core, beside = neighbours(w, (m, now), r, edge_low, edge_high, nx)
                fresh = keep * core + spread * beside
                if r == 1:
                    fresh = came[m][depth] * fresh
                else:
                    fresh = half_of(m, r, kinds[s]) * fresh
                if r >= depth:
                    at = place(m, r)
                    product = fresh * margin[s, upper[m] * depth + r - depth].astype(jnp.float32)
                    edge_dens[upper[m] * depth + r - depth, kinds[s]] += product
                    total[...] += folded(product)
                    if s == rest:
                        last[upper[m] * depth + at - upper[m] * (planes - depth)] = fresh.astype(
                            jnp.bfloat16
                        )
                elif m == 0:
                    fresh = inside * fresh
                if s < rest:
                    if r > 1:
                        fresh = half_of(m, r, kinds[s + 1]) * fresh
                    w[m, later, r, rows, :] = fresh
        if s == 0:
            part = jnp.sum(inner_sums[0] + total[...], axis=0, keepdims=True)
    whole = jnp.sum(inner_sums[1] + total[...], axis=0, keepdims=True)
    both = jnp.concatenate([part, whole], 0)
    sums[...] = jnp.broadcast_to(both[None], sums.shape)


def weigh_kernel(cells, params, sums, dens, edge_dens, out):
    planes, _, nx, ny = dens.shape
    depth = edge_dens.shape[0] // 2
    both = jnp.sum(sums[...], axis=0)
    partition = jnp.sum(both[0:1]) / cells
    weight = params[1:2] / splat(partition)
    level = weight * (jnp.sum(both[1:2]) / cells)
    shift = level * (stiffness / (flory_chi + 2.0 * stiffness))

    for p in range(planes):
        for t in range(2):
            if p < depth:
                mine = edge_dens[p, t]
            elif p >= planes - depth:
                mine = edge_dens[depth + planes - 1 - p, t]
            else:
                mine = dens[p, t]
            out[p, t * nx : (t + 1) * nx, :] = weight * mine - shift


def reduce_kernel(arrived, out):
    acc = arrived[0]
    for c in range(1, arrived.shape[0]):
        acc = acc + arrived[c]
    out[...] = acc


def spread_kernel(pair, blocks):
    both = pair[0] + pair[1]
    blocks[...] = jnp.broadcast_to(both[None], blocks.shape)


def update_kernel(blocks, fields, middle, last, out, final, fresh, sems, end_sems):
    _, planes, nx, ny = fields.shape
    chunk = planes // sems.shape[0]
    depth = last.shape[0] // 2
    parts = (
        (middle, depth, middle.shape[0]),
        (last.at[pl.ds(0, depth)], 0, depth),
        (last.at[pl.ds(depth, depth)], planes - depth, depth),
    )
    copies = []
    for i, (part, at, count) in enumerate(parts):
        copies.append(pltpu.make_async_copy(part, final.at[pl.ds(at, count)], end_sems.at[i]))
        copies[-1].start()
    for i in range(sems.shape[0]):
        for p in range(i * chunk, (i + 1) * chunk):
            first, second = blocks[p, 0:nx, :], blocks[p, nx : 2 * nx, :]
            pressure = stiffness * (first + second)
            old = fields[0, p]
            fresh[0, p] = old + mixing * (flory_chi * second + pressure - old)
            old = fields[1, p]
            fresh[1, p] = old + mixing * (flory_chi * first + pressure - old)
        at = pl.ds(i * chunk, chunk)
        for t in range(2):
            copy = pltpu.make_async_copy(fresh.at[t, at], out.at[t, at], sems.at[i, t])
            copy.start()
            copies.append(copy)
    for copy in copies:
        copy.wait()


def call(kernel, outs, scratch, args, smem, flops, name, vmem=2, hbm=0, kinds=False, far=()):
    size = sum(a.size * a.dtype.itemsize for a in args) + sum(
        o.size * o.dtype.itemsize for o in outs
    )
    anywhere = pl.BlockSpec(memory_space=pltpu.HBM)
    return pl.pallas_call(
        kernel,
        out_shape=outs,
        in_specs=[SMEM] * smem + [VMEM] * (len(args) - smem - hbm) + [anywhere] * hbm,
        out_specs=[anywhere if i in far else VMEM for i in range(len(outs) - kinds)]
        + [SMEM] * kinds,
        scratch_shapes=scratch,
        compiler_params=pltpu.CompilerParams(vmem_limit_bytes=vmem * 2**20),
        cost_estimate=pl.CostEstimate(flops=flops, bytes_accessed=size, transcendentals=0),
        name=name,
    )(*args)


def in_hbm(x):
    return pltpu.with_memory_space_constraint(x, pltpu.HBM)


def f32(*shape):
    return jax.ShapeDtypeStruct(shape, jnp.float32)


def body(q_init, q_back, fields, lengths, counts, types):
    _, planes, nx, ny = q_init.shape
    depth = q_back.shape[1]
    cells = float(lax.axis_size(SLAB) * planes * nx * ny)
    q, back = q_init[0], q_back[0]
    types = types.T
    peers = lax.axis_size(XY)
    slabs = lax.axis_size(SLAB)
    message = f32(3 * depth - 3, nx, ny)
    classes = lengths.shape[0]

    outward, inward, params, kinds = call(
        edges_kernel,
        [message, message, f32(8, ny), jax.ShapeDtypeStruct((depth,), jnp.int32)],
        [
            pltpu.VMEM((2, depth, nx, ny), jnp.bfloat16),
            pltpu.VMEM((2, 4, nx, ny), jnp.float32),
            pltpu.SMEM((classes,), jnp.int32),
            pltpu.SMEM((classes,), jnp.int32),
            pltpu.SMEM((depth, classes), jnp.int32),
            pltpu.SemaphoreType.DMA((6 * depth + 3,)),
        ],
        tuple(map(in_hbm, (lengths, counts, types, q, fields))),
        0,
        10**6,
        "edges",
        vmem=4,
        hbm=5,
        kinds=True,
    )
    across = [(i, i + 1) for i in range(1, slabs - 1, 2)]
    within = [(i, i + 1) for i in range(0, slabs, 2)]
    outer = lax.ppermute(outward, SLAB, across + [(b, a) for a, b in across])
    near = lax.ppermute(inward, SLAB, within + [(b, a) for a, b in within])

    padded = nx + 2 * TOP
    half, state, dens, middle, sums, margin = call(
        inner_kernel,
        [
            f32(2, planes, nx, ny),
            f32(depth, 4, nx, ny),
            f32(planes, 2, nx, ny),
            jax.ShapeDtypeStruct((planes - 2 * depth, nx, ny), jnp.bfloat16),
            f32(2, 8, ny),
            jax.ShapeDtypeStruct((depth, 2 * depth, nx, ny), back.dtype),
        ],
        [
            pltpu.VMEM((2, planes, padded, ny), jnp.float32),
            pltpu.VMEM((8, ny), jnp.float32),
            pltpu.VMEM(back.shape, back.dtype),
            pltpu.SemaphoreType.DMA((depth,)),
        ],
        (kinds, params, q, fields, in_hbm(back)),
        1,
        10**8,
        "inner",
        vmem=8,
        hbm=1,
    )
    last, edge_dens, sums = call(
        outer_kernel,
        [
            jax.ShapeDtypeStruct((2 * depth, nx, ny), jnp.bfloat16),
            f32(2 * depth, 2, nx, ny),
            f32(slabs, 2, ny),
        ],
        [
            pltpu.VMEM((2, 2, 2 * depth + 2, padded, ny), jnp.float32),
            pltpu.VMEM((8, ny), jnp.float32),
        ],
        (kinds, params, outer, near, half, state, dens, sums, margin),
        1,
        10**8,
        "outer",
        vmem=8,
    )
    sums = lax.all_to_all(sums, SLAB, 0, 0, tiled=True)
    (sent,) = call(
        functools.partial(weigh_kernel, cells),
        [f32(peers, 2 * nx, ny)],
        [],
        (params, sums, dens, edge_dens),
        0,
        10**6,
        "weigh",
        vmem=8,
    )
    arrived = lax.all_to_all(sent, XY, 0, 0, tiled=True)
    (own,) = call(reduce_kernel, [f32(2 * nx, ny)], [], (arrived,), 0, 10**6, "reduce", vmem=8)
    pair = lax.all_gather(own, "zh", axis=0, tiled=False)
    (blocks,) = call(
        spread_kernel, [f32(peers, 2 * nx, ny)], [], (pair,), 0, 10**6, "spread", vmem=8
    )
    blocks = lax.all_to_all(blocks, XY, 0, 0, tiled=True)
    fields_new, final = call(
        update_kernel,
        [f32(2, planes, nx, ny), jax.ShapeDtypeStruct((planes, nx, ny), jnp.bfloat16)],
        [
            pltpu.VMEM((2, planes, nx, ny), jnp.float32),
            pltpu.SemaphoreType.DMA((4, 2)),
            pltpu.SemaphoreType.DMA((3,)),
        ],
        (blocks, fields, middle, last),
        0,
        10**6,
        "update",
        vmem=8,
        far=(0, 1),
    )
    return fields_new, final[None]


def solution(mesh):
    finer = Mesh(mesh.devices.reshape(2, 4, 4, mesh.shape["slab"]), ("zh", "y", "x", SLAB))
    in_specs = (
        P(CLS, SLAB, None, None),
        P(CLS, None, SLAB, None, None),
        P(None, SLAB, None, None),
        P(),
        P(),
        P(),
    )
    out_specs = (P(None, SLAB, None, None), P(CLS, SLAB, None, None))
    return jax.shard_map(body, mesh=finer, in_specs=in_specs, out_specs=out_specs, check_vma=False)
```

```python
import functools

import jax
import jax.numpy as jnp
from jax import lax
from jax.experimental import pallas as pl
from jax.experimental.pallas import tpu as pltpu
from jax.sharding import Mesh
from jax.sharding import PartitionSpec as P

CLS = ("zh", "y", "x")
XY = ("x", "y")
SLAB = "slab"

flory_chi = 2.0
stiffness = 1.0
mixing = 0.5
diffusion_scale = 0.125

VMEM = pl.BlockSpec(memory_space=pltpu.VMEM)
SMEM = pl.BlockSpec(memory_space=pltpu.SMEM)
UNROLL = True
TOP = 8


def own_class():
    return (lax.axis_index("zh") * 4 + lax.axis_index("y")) * 4 + lax.axis_index("x")


def splat(value, shape=(1, 128)):
    return jnp.full(shape, value, jnp.float32)


def folded(plane):
    return jnp.sum(plane.reshape(-1, 8, plane.shape[-1]), axis=0)


def neighbours(w, at, p, lane_low, lane_high, nx):
    core = w[(*at, p, slice(TOP, TOP + nx))]
    total = w[(*at, p - 1, slice(TOP, TOP + nx))] + w[(*at, p + 1, slice(TOP, TOP + nx))]
    total = total + w[(*at, p, slice(TOP - 1, TOP + nx - 1))]
    total = total + w[(*at, p, slice(TOP + 1, TOP + nx + 1))]
    ny = core.shape[-1]
    before = jnp.where(lane_low, 0.0, pltpu.roll(core, 1, 1))
    after = jnp.where(lane_high, 0.0, pltpu.roll(core, ny - 1, 1))
    return core, total + before + after


def lane_edges(nx, ny):
    lane = lax.broadcasted_iota(jnp.int32, (nx, ny), 1)
    return lane == 0, lane == ny - 1


def clear_margins(w, nx):
    blank = jnp.zeros(w.shape[:2] + (TOP, w.shape[-1]), jnp.float32)
    w[:, :, 0:TOP, :] = blank
    w[:, :, TOP + nx : TOP + nx + TOP, :] = blank


def sides():
    core = lax.rem(lax.axis_index(SLAB), 2)
    return core, 1 - core


def edges_kernel(
    lengths,
    counts,
    types,
    q,
    fields,
    outward,
    inward,
    params,
    kinds,
    ends,
    raw,
    own_lengths,
    own_counts,
    own_types,
    sems,
):
    planes = q.shape[0]
    depth = types.shape[0]
    cls = own_class()
    copies = [(lengths, own_lengths), (counts, own_counts), (types, own_types)]
    for side, start in enumerate((0, planes - depth)):
        copies.append((q.at[pl.ds(start, depth)], ends.at[side]))
        copies.append((fields.at[:, pl.ds(start, depth)], raw.at[side]))
    copies = [pltpu.make_async_copy(a, b, sems.at[i]) for i, (a, b) in enumerate(copies)]
    for copy in copies:
        copy.start()
    for copy in copies[:3]:
        copy.wait()
    whole = own_lengths[0]
    for c in range(1, own_lengths.shape[0]):
        whole = whole + own_lengths[c]
    length = splat(own_lengths[cls].astype(jnp.float32))
    size = length / splat(own_counts[cls].astype(jnp.float32))
    fraction = length / splat(whole.astype(jnp.float32))
    params[0:1] = size
    params[1:2] = fraction * size
    for s in range(depth):
        kinds[s] = own_types[s, cls]
    first, second = own_types[0, cls], own_types[1, cls]
    scale = -0.5 * size
    for copy in copies[3:]:
        copy.wait()
    for message, upper in zip((outward, inward), sides()):
        for r in range(depth):
            at = upper * r + (1 - upper) * (depth - 1 - r)
            chosen = raw[upper, first, at]
            message[r] = jnp.exp(scale * chosen) * ends[upper, at].astype(jnp.float32)
            if r == 1:
                message[depth] = jnp.exp(scale * (chosen + raw[upper, second, at]))
            elif r > 1:
                for t in range(2):
                    message[depth + 1 + 2 * (r - 2) + t] = raw[upper, t, at]


def inner_kernel(
    kinds, params, q, fields, source, half, state, dens, middle, sums, margin, w, total, back, sems
):
    planes, nx, ny = q.shape
    depth = back.shape[0]
    copies = [pltpu.make_async_copy(source.at[s], back.at[s], sems.at[s]) for s in range(depth)]
    for copy in copies:
        copy.start()
    size = params[0:1]
    spread = diffusion_scale * size
    keep = 1.0 - 6.0 * spread
    scale = -0.5 * size
    kinds = [kinds[s] for s in range(depth)]
    edge_low, edge_high = lane_edges(nx, ny)
    clear_margins(w, nx)
    total[...] = jnp.zeros_like(total)
    rows = slice(TOP, TOP + nx)

    def first(p, carry):
        half[0, p] = jnp.exp(scale * fields[0, p])
        half[1, p] = jnp.exp(scale * fields[1, p])
        w[0, p, rows, :] = half[kinds[0], p] * q[p].astype(jnp.float32)
        dens[p, 0] = jnp.zeros((nx, ny), jnp.float32)
        dens[p, 1] = jnp.zeros((nx, ny), jnp.float32)
        return carry

    lax.fori_loop(0, planes, first, 0, unroll=2)

    for s in range(depth):
        now, later = s % 2, (s + 1) % 2
        kind = kinds[s]
        last = s == depth - 1
        copies[s].wait()
        for i, p in enumerate((s, s + 1, planes - 1 - s, planes - 2 - s)):
            state[s, i] = w[now, p, rows, :]

        def each(p, carry):
            core, beside = neighbours(w, (now,), p, edge_low, edge_high, nx)
            fresh = half[kind, p] * (keep * core + spread * beside)
            product = fresh * back[s, p].astype(jnp.float32)
            dens[p, kind] += product
            total[...] += folded(product)
            if last:
                middle[p - depth] = fresh.astype(jnp.bfloat16)
            else:
                w[later, p, rows, :] = half[kinds[s + 1], p] * fresh
            return carry

        lax.fori_loop(s + 1, planes - 1 - s, each, 0, unroll=UNROLL)
        if s == 0:
            sums[0] = total[...]
        for p in range(depth):
            margin[s, p] = back[s, p]
            margin[s, depth + p] = back[s, planes - 1 - p]
    sums[1] = total[...]


def outer_kernel(
    kinds,
    params,
    outer,
    near,
    half,
    state,
    dens,
    inner_sums,
    margin,
    last,
    edge_dens,
    sums,
    w,
    total,
):
    _, planes, nx, ny = half.shape
    depth = margin.shape[0]
    slab = lax.axis_index(SLAB)
    inside = jnp.logical_and(slab > 0, slab < lax.axis_size(SLAB) - 1)
    inside = splat(jnp.where(inside, 1.0, 0.0))
    size = params[0:1]
    spread = diffusion_scale * size
    keep = 1.0 - 6.0 * spread
    scale = -0.5 * size
    kinds = [kinds[s] for s in range(depth)]
    edge_low, edge_high = lane_edges(nx, ny)
    for side in range(2):
        clear_margins(w.at[side], nx)
    total[...] = jnp.zeros_like(total)
    rows = slice(TOP, TOP + nx)
    came = (outer, near)
    rest = depth - 1
    upper = sides()

    def place(m, r):
        return upper[m] * (planes - 1) + (1 - 2 * upper[m]) * (r - depth)

    def half_of(m, r, kind):
        if r >= depth:
            return half[kind, place(m, r)]
        return jnp.exp(scale * came[m][depth + 1 + 2 * (r - 2) + kind])

    for m in range(2):
        for r in range(depth):
            w[m, 0, r, rows, :] = came[m][r]
        for p in range(depth):
            for t in range(2):
                edge_dens[upper[m] * depth + p, t] = dens[place(m, depth + p), t]

    for s in range(depth):
        now, later = s % 2, (s + 1) % 2
        for m in range(2):
            for i in range(2):
                w[m, now, s + depth + i, rows, :] = state[s, 2 * upper[m] + i]
        for i in range(depth):
            for m in range(2):
                r = s + 1 + i
                core, beside = neighbours(w, (m, now), r, edge_low, edge_high, nx)
                fresh = keep * core + spread * beside
                if r == 1:
                    fresh = came[m][depth] * fresh
                else:
                    fresh = half_of(m, r, kinds[s]) * fresh
                if r >= depth:
                    at = place(m, r)
                    product = fresh * margin[s, upper[m] * depth + r - depth].astype(jnp.float32)
                    edge_dens[upper[m] * depth + r - depth, kinds[s]] += product
                    total[...] += folded(product)
                    if s == rest:
                        last[upper[m] * depth + at - upper[m] * (planes - depth)] = fresh.astype(
                            jnp.bfloat16
                        )
                elif m == 0:
                    fresh = inside * fresh
                if s < rest:
                    if r > 1:
                        fresh = half_of(m, r, kinds[s + 1]) * fresh
                    w[m, later, r, rows, :] = fresh
        if s == 0:
            part = jnp.sum(inner_sums[0] + total[...], axis=0, keepdims=True)
    whole = jnp.sum(inner_sums[1] + total[...], axis=0, keepdims=True)
    both = jnp.concatenate([part, whole], 0)
    sums[...] = jnp.broadcast_to(both[None], sums.shape)


def weigh_kernel(cells, params, sums, dens, edge_dens, out):
    planes, _, nx, ny = dens.shape
    depth = edge_dens.shape[0] // 2
    both = jnp.sum(sums[...], axis=0)
    partition = jnp.sum(both[0:1]) / cells
    weight = params[1:2] / splat(partition)
    level = weight * (jnp.sum(both[1:2]) / cells)
    shift = level * (stiffness / (flory_chi + 2.0 * stiffness))

    for p in range(planes):
        for t in range(2):
            if p < depth:
                mine = edge_dens[p, t]
            elif p >= planes - depth:
                mine = edge_dens[depth + planes - 1 - p, t]
            else:
                mine = dens[p, t]
            out[p, t * nx : (t + 1) * nx, :] = weight * mine - shift


def reduce_kernel(arrived, out):
    acc = arrived[0]
    for c in range(1, arrived.shape[0]):
        acc = acc + arrived[c]
    out[...] = acc


def spread_kernel(pair, blocks):
    both = pair[0] + pair[1]
    blocks[...] = jnp.broadcast_to(both[None], blocks.shape)


def update_kernel(blocks, fields, middle, last, out, final, fresh, sems, end_sems):
    _, planes, nx, ny = fields.shape
    chunk = planes // sems.shape[0]
    depth = last.shape[0] // 2
    parts = (
        (middle, depth, middle.shape[0]),
        (last.at[pl.ds(0, depth)], 0, depth),
        (last.at[pl.ds(depth, depth)], planes - depth, depth),
    )
    copies = []
    for i, (part, at, count) in enumerate(parts):
        copies.append(pltpu.make_async_copy(part, final.at[pl.ds(at, count)], end_sems.at[i]))
        copies[-1].start()
    for i in range(sems.shape[0]):
        for p in range(i * chunk, (i + 1) * chunk):
            first, second = blocks[p, 0:nx, :], blocks[p, nx : 2 * nx, :]
            pressure = stiffness * (first + second)
            old = fields[0, p]
            fresh[0, p] = old + mixing * (flory_chi * second + pressure - old)
            old = fields[1, p]
            fresh[1, p] = old + mixing * (flory_chi * first + pressure - old)
        at = pl.ds(i * chunk, chunk)
        for t in range(2):
            copy = pltpu.make_async_copy(fresh.at[t, at], out.at[t, at], sems.at[i, t])
            copy.start()
            copies.append(copy)
    for copy in copies:
        copy.wait()


def call(kernel, outs, scratch, args, smem, flops, name, vmem=2, hbm=0, kinds=False, far=()):
    size = sum(a.size * a.dtype.itemsize for a in args) + sum(
        o.size * o.dtype.itemsize for o in outs
    )
    anywhere = pl.BlockSpec(memory_space=pltpu.HBM)
    return pl.pallas_call(
        kernel,
        out_shape=outs,
        in_specs=[SMEM] * smem + [VMEM] * (len(args) - smem - hbm) + [anywhere] * hbm,
        out_specs=[anywhere if i in far else VMEM for i in range(len(outs) - kinds)]
        + [SMEM] * kinds,
        scratch_shapes=scratch,
        compiler_params=pltpu.CompilerParams(vmem_limit_bytes=vmem * 2**20),
        cost_estimate=pl.CostEstimate(flops=flops, bytes_accessed=size, transcendentals=0),
        name=name,
    )(*args)


def in_hbm(x):
    return pltpu.with_memory_space_constraint(x, pltpu.HBM)


def f32(*shape):
    return jax.ShapeDtypeStruct(shape, jnp.float32)


def body(q_init, q_back, fields, lengths, counts, types):
    _, planes, nx, ny = q_init.shape
    depth = q_back.shape[1]
    cells = float(lax.axis_size(SLAB) * planes * nx * ny)
    q, back = q_init[0], q_back[0]
    types = types.T
    peers = lax.axis_size(XY)
    slabs = lax.axis_size(SLAB)
    message = f32(3 * depth - 3, nx, ny)
    classes = lengths.shape[0]

    outward, inward, params, kinds = call(
        edges_kernel,
        [message, message, f32(8, ny), jax.ShapeDtypeStruct((depth,), jnp.int32)],
        [
            pltpu.VMEM((2, depth, nx, ny), jnp.bfloat16),
            pltpu.VMEM((2, 2, depth, nx, ny), jnp.float32),
            pltpu.SMEM((classes,), jnp.int32),
            pltpu.SMEM((classes,), jnp.int32),
            pltpu.SMEM((depth, classes), jnp.int32),
            pltpu.SemaphoreType.DMA((7,)),
        ],
        tuple(map(in_hbm, (lengths, counts, types, q, fields))),
        0,
        10**6,
        "edges",
        vmem=4,
        hbm=5,
        kinds=True,
    )
    across = [(i, i + 1) for i in range(1, slabs - 1, 2)]
    within = [(i, i + 1) for i in range(0, slabs, 2)]
    outer = lax.ppermute(outward, SLAB, across + [(b, a) for a, b in across])
    near = lax.ppermute(inward, SLAB, within + [(b, a) for a, b in within])

    padded = nx + 2 * TOP
    half, state, dens, middle, sums, margin = call(
        inner_kernel,
        [
            f32(2, planes, nx, ny),
            f32(depth, 4, nx, ny),
            f32(planes, 2, nx, ny),
            jax.ShapeDtypeStruct((planes - 2 * depth, nx, ny), jnp.bfloat16),
            f32(2, 8, ny),
            jax.ShapeDtypeStruct((depth, 2 * depth, nx, ny), back.dtype),
        ],
        [
            pltpu.VMEM((2, planes, padded, ny), jnp.float32),
            pltpu.VMEM((8, ny), jnp.float32),
            pltpu.VMEM(back.shape, back.dtype),
            pltpu.SemaphoreType.DMA((depth,)),
        ],
        (kinds, params, q, fields, in_hbm(back)),
        1,
        10**8,
        "inner",
        vmem=8,
        hbm=1,
    )
    last, edge_dens, sums = call(
        outer_kernel,
        [
            jax.ShapeDtypeStruct((2 * depth, nx, ny), jnp.bfloat16),
            f32(2 * depth, 2, nx, ny),
            f32(slabs, 2, ny),
        ],
        [
            pltpu.VMEM((2, 2, 2 * depth + 2, padded, ny), jnp.float32),
            pltpu.VMEM((8, ny), jnp.float32),
        ],
        (kinds, params, outer, near, half, state, dens, sums, margin),
        1,
        10**8,
        "outer",
        vmem=8,
    )
    sums = lax.all_to_all(sums, SLAB, 0, 0, tiled=True)
    (sent,) = call(
        functools.partial(weigh_kernel, cells),
        [f32(peers, 2 * nx, ny)],
        [],
        (params, sums, dens, edge_dens),
        0,
        10**6,
        "weigh",
        vmem=8,
    )
    arrived = lax.all_to_all(sent, XY, 0, 0, tiled=True)
    (own,) = call(reduce_kernel, [f32(2 * nx, ny)], [], (arrived,), 0, 10**6, "reduce", vmem=8)
    pair = lax.all_gather(own, "zh", axis=0, tiled=False)
    (blocks,) = call(
        spread_kernel, [f32(peers, 2 * nx, ny)], [], (pair,), 0, 10**6, "spread", vmem=8
    )
    blocks = lax.all_to_all(blocks, XY, 0, 0, tiled=True)
    fields_new, final = call(
        update_kernel,
        [f32(2, planes, nx, ny), jax.ShapeDtypeStruct((planes, nx, ny), jnp.bfloat16)],
        [
            pltpu.VMEM((2, planes, nx, ny), jnp.float32),
            pltpu.SemaphoreType.DMA((4, 2)),
            pltpu.SemaphoreType.DMA((3,)),
        ],
        (blocks, fields, middle, last),
        0,
        10**6,
        "update",
        vmem=8,
        far=(0, 1),
    )
    return fields_new, final[None]


def solution(mesh):
    finer = Mesh(mesh.devices.reshape(2, 4, 4, mesh.shape["slab"]), ("zh", "y", "x", SLAB))
    in_specs = (
        P(CLS, SLAB, None, None),
        P(CLS, None, SLAB, None, None),
        P(None, SLAB, None, None),
        P(),
        P(),
        P(),
    )
    out_specs = (P(None, SLAB, None, None), P(CLS, SLAB, None, None))
    return jax.shard_map(body, mesh=finer, in_specs=in_specs, out_specs=out_specs, check_vma=False)
```
